32 devices in a mesh: lat: 4 (over z), lon: 8 (over y, x, core).
Axes of the slice: x: 2, y: 2, z: 4, core: 2. Of those that a mesh axis runs over, the one named last changes fastest.
Arguments:
- layer_input: float32 [4, 768, 90, 180], P('lat', 'lon'), may hold values from -6 to 6
- grad_output: float32 [4, 768, 90, 180], P('lat', 'lon'), may hold values from -6 to 6
- first_weight: float32 [2, 8, 96, 96], replicated, may hold values from -0.625 to 0.625
- first_bias: float32 [2, 8, 96], replicated, may hold values from -3 to 3
- second_weight: float32 [2, 8, 96, 96], replicated, may hold values from -0.625 to 0.625
- second_bias: float32 [2, 8, 96], replicated, may hold values from -3 to 3
Outputs:
- grad_input: float32 [4, 768, 90, 180], P('lat', 'lon')
- grad_first_weight: float32 [2, 8, 96, 96], replicated
- grad_first_bias: float32 [2, 8, 96], replicated
- grad_second_weight: float32 [2, 8, 96, 96], replicated
- grad_second_bias: float32 [2, 8, 96], replicated
The draws below stay inside these ranges and needn't reach their ends.
All inputs are finite; a program needn't handle non-finite values.
Results may differ from the reference program's by a relative error of at most 0.0003.
Values sent between devices are 32-bit elements; how exact they have to be, the bound alone decides.
No kernel may reach another device: no remote copies, remote signals or barrier semaphores. Data moves between devices by JAX's collectives and lax.ppermute only.
A program may use at most 192 MiB of HBM per device.

```python
import jax
import jax.numpy as jnp
from jax import lax

H = 90
W = 180
BS = 96
NB = 8
B = 4
C = 768


def block_levels(own_key, extent, shards, smallest, top_value):
    factor_of, own = 1.0, jax.random.fold_in(own_key, 6)
    for axis_at, shards_of in shards:
        heights = jnp.exp(jax.random.uniform(jax.random.fold_in(own, axis_at), (shards_of,), jnp.float32, smallest / len(shards), top_value / len(shards)))
        factor_of = factor_of * jnp.repeat(heights, extent[axis_at] // shards_of).reshape([-1 if axis == axis_at else 1 for axis in range(len(extent))])
    return factor_of


def noise(rng, extent, deviation, most, cuts=(), kind=jnp.bfloat16):
    drawn = deviation * jax.random.normal(rng, extent, jnp.float32)
    if cuts:
        drawn = drawn * block_levels(rng, extent, cuts, -0.22, 0.18)
    return jnp.clip(drawn, -most, most).astype(kind)


def setup_inputs(seed: int = 0) -> dict:
    arg_keys = jax.random.split(jax.random.key(seed), 7)
    return {
        "layer_input": noise(arg_keys[0], (B, C, H, W), 1.0, 6.0, ((0, 4), (1, 8)), jnp.float32),
        "grad_output": noise(arg_keys[1], (B, C, H, W), 1.0, 6.0, ((0, 4), (1, 8)), jnp.float32),
        "first_weight": noise(arg_keys[2], (2, NB, BS, BS), BS ** -0.5, 0.625, (), jnp.float32),
        "first_bias": noise(arg_keys[3], (2, NB, BS), 0.5, 3.0, (), jnp.float32),
        "second_weight": noise(arg_keys[4], (2, NB, BS, BS), BS ** -0.5, 0.625, (), jnp.float32),
        "second_bias": noise(arg_keys[5], (2, NB, BS), 0.5, 3.0, (), jnp.float32),
    }


SHRINK = 0.01

def mix(left, mat):
    return jnp.einsum('bchk,cd->bdhk', left, mat, precision=lax.Precision.HIGHEST)

def spread(vector):
    return vector[None, :, None, None]

def forward_block(field, w_one, b_one, w_two, b_two):
    spectrum = jnp.fft.rfft2(field, axes=(2, 3), norm='ortho')
    x_real = jnp.real(spectrum)
    x_imag = jnp.imag(spectrum)
    a_real = mix(x_real, w_one[0]) - mix(x_imag, w_one[1]) + spread(b_one[0])
    a_imag = mix(x_imag, w_one[0]) + mix(x_real, w_one[1]) + spread(b_one[1])
    o_real = jax.nn.gelu(a_real, approximate=True)
    o_imag = jax.nn.gelu(a_imag, approximate=True)
    z_real = mix(o_real, w_two[0]) - mix(o_imag, w_two[1]) + spread(b_two[0])
    z_imag = mix(o_imag, w_two[0]) + mix(o_real, w_two[1]) + spread(b_two[1])
    s_real = z_real - SHRINK * jnp.tanh(z_real / SHRINK)
    s_imag = z_imag - SHRINK * jnp.tanh(z_imag / SHRINK)
    return jnp.fft.irfft2(s_real + 1j * s_imag, s=(H, W), axes=(2, 3), norm='ortho')

def one_block(packed):
    field, cotangent, w_one, b_one, w_two, b_two = packed
    _, pullback = jax.vjp(forward_block, field, w_one, b_one, w_two, b_two)
    return pullback(cotangent)

def reference(layer_input, grad_output, first_weight, first_bias, second_weight, second_bias):
    fields = jnp.moveaxis(layer_input.reshape(B, NB, BS, H, W), 1, 0)
    cotangents = jnp.moveaxis(grad_output.reshape(B, NB, BS, H, W), 1, 0)
    results = lax.map(one_block, (fields, cotangents, jnp.moveaxis(first_weight, 1, 0), jnp.moveaxis(first_bias, 1, 0), jnp.moveaxis(second_weight, 1, 0), jnp.moveaxis(second_bias, 1, 0)))
    grad_field, grad_w_one, grad_b_one, grad_w_two, grad_b_two = results
    grad_input = jnp.moveaxis(grad_field, 0, 1).reshape(B, C, H, W)
    return (grad_input, jnp.moveaxis(grad_w_one, 0, 1), jnp.moveaxis(grad_b_one, 0, 1), jnp.moveaxis(grad_w_two, 0, 1), jnp.moveaxis(grad_b_two, 0, 1))
```

```python
import math

import jax
import jax.numpy as jnp
from jax import lax
from jax.sharding import PartitionSpec as P

SHRINK = 0.01
GELU_SCALE = math.sqrt(2.0 / math.pi)
GELU_CUBE = 0.044715
PREC = lax.Precision.HIGH


def tables(length, count, limit):
    first = jnp.arange(length, dtype=jnp.int32)[:, None]
    second = jnp.arange(count, dtype=jnp.int32)[None, :]
    angle = 2.0 * math.pi / length * (first * second % length).astype(jnp.float32)
    keeper = (second < limit).astype(jnp.float32) / math.sqrt(length)
    return (jnp.cos(angle) * keeper, jnp.sin(angle) * keeper)


def cotangent_weight(length, count):
    index = jnp.arange(count, dtype=jnp.int32)
    edge = (index == 0) | (2 * index == length)
    return jnp.where(edge, 1.0, 2.0).astype(jnp.float32)


def gelu_slope(value):
    inner = GELU_SCALE * (value + GELU_CUBE * value * value * value)
    tangent = jnp.tanh(inner)
    return 0.5 * (1.0 + tangent) + 0.5 * value * (1.0 - tangent * tangent) * GELU_SCALE * (
        1.0 + 3.0 * GELU_CUBE * value * value
    )


def complex_matrix(weight):
    real_part = weight[0]
    imag_part = weight[1]
    upper = jnp.stack([real_part, imag_part], axis=1)
    lower = jnp.stack([-imag_part, real_part], axis=1)
    return jnp.stack([upper, lower], axis=0)


def forward_mix(left, matrix):
    return jnp.einsum("psir,piqj->qsjr", left, matrix, precision=PREC)


def back_mix(left, matrix):
    return jnp.einsum("qsjr,piqj->psir", left, matrix, precision=PREC)


def weight_grad(left, right):
    total = jnp.einsum("psir,qsjr->piqj", left, right, precision=PREC)
    return jnp.stack(
        [total[0, :, 0, :] + total[1, :, 1, :], total[0, :, 1, :] - total[1, :, 0, :]]
    )


def bias_view(vector):
    return vector[:, None, :, None]


def block_backward(x_both, g_both, first_weight, first_bias, second_weight, second_bias):
    first_matrix = complex_matrix(first_weight)
    second_matrix = complex_matrix(second_weight)
    a_both = forward_mix(x_both, first_matrix) + bias_view(first_bias)
    o_both = jax.nn.gelu(a_both, approximate=True)
    z_both = forward_mix(o_both, second_matrix) + bias_view(second_bias)
    e_both = g_both * jnp.tanh(z_both / SHRINK) ** 2
    grad_w_two = weight_grad(o_both, e_both)
    grad_b_two = jnp.sum(e_both, axis=(1, 3))
    s_both = back_mix(e_both, second_matrix) * gelu_slope(a_both)
    grad_w_one = weight_grad(x_both, s_both)
    grad_b_one = jnp.sum(s_both, axis=(1, 3))
    d_both = back_mix(s_both, first_matrix)
    return d_both, (grad_w_one, grad_b_one, grad_w_two, grad_b_two)


def on_device(layer_input, grad_output, first_weight, first_bias, second_weight, second_bias):
    lon_count = lax.axis_size("lon")
    samples, local_ch, lat_rows, lon_cols = layer_input.shape
    blocks, width = first_weight.shape[1], first_weight.shape[2]
    group = width // local_ch
    groups = [list(range(at, at + group)) for at in range(0, lon_count, group)]
    block = lax.axis_index("lon") // group
    kept_freqs = lon_cols // 2 + 1
    freq_slots = -(-kept_freqs // group) * group
    lon_cos, lon_sin = tables(lon_cols, freq_slots, kept_freqs)
    factor_row = cotangent_weight(lon_cols, freq_slots)[None, :]
    lon_table = jnp.stack([lon_cos, -lon_sin], axis=1)
    cot_table = jnp.stack([lon_cos * factor_row, -lon_sin * factor_row], axis=1)
    lon_back = jnp.stack([lon_cos.T, -lon_sin.T])
    lat_cos, lat_sin = tables(lat_rows, lat_rows, lat_rows)
    lat_table = jnp.stack(
        [jnp.stack([lat_cos, -lat_sin], axis=1), jnp.stack([lat_sin, lat_cos], axis=1)]
    )
    lat_back = jnp.stack(
        [jnp.stack([lat_cos, lat_sin], axis=1), jnp.stack([-lat_sin, lat_cos], axis=1)]
    )

    def spectrum(data, table):
        half = jnp.einsum("schw,wqk->qsckh", data, table, precision=PREC)
        full = jnp.einsum("psckh,phqm->qsckm", half, lat_table, precision=PREC)
        return full.reshape((2, samples, local_ch, freq_slots * lat_rows))

    def share(data, split, concat):
        if group == 1:
            return data
        return lax.all_to_all(
            data, "lon", split_axis=split, concat_axis=concat, axis_index_groups=groups, tiled=True
        )

    x_modes = share(spectrum(layer_input, lon_table), 3, 2)
    g_modes = share(spectrum(grad_output, cot_table), 3, 2)

    def mine(weight):
        return lax.dynamic_index_in_dim(weight, block, axis=1, keepdims=False)

    d_modes, partial_grads = block_backward(
        x_modes, g_modes, mine(first_weight), mine(first_bias), mine(second_weight), mine(second_bias)
    )
    flat_grads = jnp.concatenate([piece.reshape(-1) for piece in partial_grads])
    summed = lax.psum(flat_grads, "lat")
    if group > 1:
        summed = lax.psum(summed, "lon", axis_index_groups=groups)
    whole = lax.all_gather(summed, "lon", axis=0, tiled=False)[::group]
    stacked = share(d_modes, 2, 3)
    shape_five = (2, samples, local_ch, freq_slots, lat_rows)
    grad_input = jnp.einsum(
        "qsckh,qkw->schw",
        jnp.einsum("psckm,pmqh->qsckh", stacked.reshape(shape_five), lat_back, precision=PREC),
        lon_back,
        precision=PREC,
    )
    results = []
    offset = 0
    for piece in partial_grads:
        part = whole[:, offset : offset + piece.size].reshape((blocks,) + piece.shape)
        results.append(jnp.moveaxis(part, 0, 1))
        offset = offset + piece.size
    grad_w_one, grad_b_one, grad_w_two, grad_b_two = results
    return (grad_input, grad_w_one, grad_b_one, grad_w_two, grad_b_two)


def solution(mesh):
    placed = (P("lat", "lon", None, None), P("lat", "lon", None, None), P(), P(), P(), P())
    return jax.shard_map(
        on_device,
        mesh=mesh,
        in_specs=placed,
        out_specs=(P("lat", "lon", None, None), P(), P(), P(), P()),
        check_vma=False,
    )
```

```python
import functools
import math

import jax
import jax.numpy as jnp
import ml_dtypes
import numpy as np
from jax import lax
from jax.experimental import pallas as pl
from jax.experimental.pallas import tpu as pltpu
from jax.sharding import PartitionSpec as P

SHRINK = 0.01
GELU_SCALE = math.sqrt(2.0 / math.pi)
GELU_CUBE = 0.044715
PRECISION = lax.Precision.HIGH
LANES = 128
SUB = 8
F32 = jnp.float32
BF16 = jnp.bfloat16
VMEM_LIMIT = 56 << 20


def round_up(value, unit):
    return -(-value // unit) * unit


def halves(table):
    high = table.astype(ml_dtypes.bfloat16)
    low = (table - high.astype(np.float64)).astype(ml_dtypes.bfloat16)
    return high, low


def split(value):
    high = value.astype(BF16)
    return high, (value - high.astype(F32)).astype(BF16)


def dot(left, right):
    return jnp.dot(left, right, preferred_element_type=F32)


def dot_tn(left, right):
    return lax.dot_general(left, right, (((0,), (0,)), ((), ())), preferred_element_type=F32)


def side_by_side(left, right):
    return jnp.concatenate([left, right], axis=1)


def trig(length, count):
    first = np.arange(count)[:, None]
    second = np.arange(length)[None, :]
    angle = 2.0 * np.pi / length * (first * second % length)
    return np.cos(angle) / math.sqrt(length), np.sin(angle) / math.sqrt(length)


class Sizes:
    def __init__(self, rows, cols):
        self.rows, self.cols = rows, cols
        self.pairs = rows // 2 + 1
        self.half = round_up(self.pairs, SUB)
        self.both = 2 * self.half
        self.freqs = cols // 2 + 1
        self.slots = round_up(self.freqs, 16)
        self.row_slots = round_up(rows, 16)
        self.col_slots = round_up(cols, 16)
        self.band = max((n for n in range(2, 7, 2) if rows % n == 0 and n * cols % SUB == 0), default=0)
        self.batch = max(n for n in range(1, 9) if self.freqs % n == 0)

    def fits(self):
        return self.band > 0 and self.batch * self.both % 16 == 0


def lat_table(size, cotangent):
    cos, sin = trig(size.rows, size.pairs)
    if cotangent:
        own = np.array([2 * m % size.rows == 0 for m in range(size.pairs)])
        cos, sin = (part * np.where(own, 0.5, 1.0)[:, None] for part in (cos, sin))
    table = np.zeros((size.both, size.row_slots))
    table[: size.pairs, : size.rows] = cos
    table[size.half : size.half + size.pairs, : size.rows] = sin
    return table


def lon_table(size, cotangent):
    cos, sin = trig(size.cols, size.freqs)
    if cotangent:
        index = np.arange(size.freqs)
        factor = np.where((index == 0) | (2 * index == size.cols), 1.0, 2.0)[:, None]
        cos, sin = cos * factor, sin * factor
    table = np.zeros((2 * size.slots, size.col_slots))
    table[: size.freqs, : size.cols] = cos
    table[size.slots : size.slots + size.freqs, : size.cols] = sin
    return table


def four_way(table):
    high, low = halves(table)
    return np.concatenate([np.concatenate([high, high], 1), np.concatenate([low, low], 1)], 0)


def stacked(table):
    return np.concatenate(halves(table), 0)


def four_product(table_ref, data):
    two = dot(table_ref[...], jnp.concatenate(split(data), axis=0))
    count = two.shape[0] // 2
    return two[:count] + two[count:]


def three_product(table_ref, high, low):
    count = table_ref.shape[0] // 2
    two = dot(table_ref[...], high)
    return two[:count] + two[count:] + dot(table_ref[:count], low)


def mix(weight_ref, which, high, low):
    return dot(high, weight_ref[which, 0]) + dot(low, weight_ref[which, 0]) + dot(high, weight_ref[which, 1])


def gradient_kernel(
    size, width, bands, batches, x_ref, g_ref, tx_ref, tg_ref, fx_ref, fg_ref, w_ref, b_ref,
    s_ref, grad_ref, fold, spectra, keep, plain, total, bias_total,
):
    step = pl.program_id(0)
    cols, slots, both, half = size.cols, size.slots, size.both, size.half
    lines = 2 * slots
    rows = size.batch * both

    @pl.when(step == 0)
    def _():
        fold[...] = jnp.zeros_like(fold)
        total[...] = jnp.zeros_like(total)
        bias_total[...] = jnp.zeros_like(bias_total)
        for which in range(2):
            spectra[which, size.rows * lines :] = jnp.zeros(((size.row_slots - size.rows) * lines, LANES), F32)

    @pl.when(step < bands)
    def _():
        for which, (field, table) in enumerate(((x_ref, tx_ref), (g_ref, tg_ref))):
            data = field.reshape(size.band * cols, width)
            for pair in range(size.band // 2):
                slot = which * (size.band // 2) + pair
                for i in range(2):
                    at = (2 * pair + i) * cols
                    high, low = split(data[at : at + cols, :])
                    fold[slot, 0, :cols, i * LANES : i * LANES + width] = high
                    fold[slot, 1, :cols, i * LANES : i * LANES + width] = low
                out = three_product(table, fold[slot, 0], fold[slot, 1])
                for i in range(2):
                    base = pl.multiple_of((step * size.band + 2 * pair + i) * lines, lines)
                    spectra[which, pl.ds(base, lines), :] = out[:, i * LANES : (i + 1) * LANES]

    @pl.when(step >= bands)
    def _():
        first = (step - bands) * size.batch
        for k in range(size.batch):
            at = k * both
            for which, table in enumerate((fx_ref, fg_ref)):
                data = side_by_side(
                    spectra[which, pl.ds(first + k, size.row_slots, stride=lines), :],
                    spectra[which, pl.ds(first + k + slots, size.row_slots, stride=lines), :],
                )
                out = four_product(table, data)
                cos_one, cos_two = out[:half, :LANES], out[:half, LANES:]
                sin_one, sin_two = out[half:, :LANES], out[half:, LANES:]
                plus = side_by_side(cos_one - sin_two, -(cos_two + sin_one))
                minus = side_by_side(cos_one + sin_two, sin_one - cos_two)
                if which == 0:
                    for part, value in ((0, plus), (1, minus)):
                        high, low = split(value)
                        here = slice(at + part * half, at + (part + 1) * half)
                        keep[0, 0, here] = high
                        keep[0, 1, here] = low
                else:
                    plain[0, at : at + half] = plus
                    plain[0, at + half : at + both] = minus
        piece = 16 * math.gcd(rows // 16, 2)

        plain[1] = mix(w_ref, 0, keep[0, 0], keep[0, 1])
        for at in range(0, rows, piece):
            here = slice(at, at + piece)
            a = plain[1, here] + b_ref[0]
            square = a * a
            tangent = jnp.tanh(a * (GELU_SCALE + (GELU_SCALE * GELU_CUBE) * square))
            part = 0.5 * a
            plain[2, here] = 0.5 + 0.5 * tangent + part * (1.0 - tangent * tangent) * (
                GELU_SCALE + (3.0 * GELU_SCALE * GELU_CUBE) * square
            )
            high, low = split(part + part * tangent)
            keep[1, 0, here] = high
            keep[1, 1, here] = low
        plain[1] = mix(w_ref, 1, keep[1, 0], keep[1, 1])
        sums = jnp.zeros((SUB, 2 * LANES), F32)
        for at in range(0, rows, piece):
            here = slice(at, at + piece)
            gate = jnp.tanh((plain[1, here] + b_ref[1]) * (1.0 / SHRINK))
            e = plain[0, here] * (gate * gate)
            for i in range(0, piece, SUB):
                sums = sums + e[i : i + SUB]
            high, low = split(e)
            keep[2, 0, here] = high
            keep[2, 1, here] = low
        bias_total[1] += sums
        plain[1] = mix(w_ref, 2, keep[2, 0], keep[2, 1])
        sums = jnp.zeros((SUB, 2 * LANES), F32)
        for at in range(0, rows, piece):
            here = slice(at, at + piece)
            s = plain[1, here] * plain[2, here]
            s_ref[here] = s
            for i in range(0, piece, SUB):
                sums = sums + s[i : i + SUB]
            high, low = split(s)
            keep[3, 0, here] = high
            keep[3, 1, here] = low
        bias_total[0] += sums
        for layer, left, right in ((0, 0, 3), (1, 1, 2)):
            total[layer] += (
                dot_tn(keep[left, 0], keep[right, 0])
                + dot_tn(keep[left, 1], keep[right, 0])
                + dot_tn(keep[left, 0], keep[right, 1])
            )

    @pl.when(step == bands + batches - 1)
    def _():
        for layer in range(2):
            upper = total[layer, :width]
            lower = total[layer, LANES : LANES + width]
            grad_ref[layer, 0, :width] = upper[:, :LANES] + lower[:, LANES:]
            grad_ref[layer, 1, :width] = upper[:, LANES:] - lower[:, :LANES]
            bias = jnp.broadcast_to(jnp.sum(bias_total[layer], axis=0, keepdims=True), (SUB, 2 * LANES))
            grad_ref[layer, 0, width:] = bias[:, :LANES]
            grad_ref[layer, 1, width:] = bias[:, LANES:]


def lat_back_kernel(size, s_ref, w_ref, f_ref, v_ref, keep, plain):
    both, half = size.both, size.half
    rows = size.batch * both
    for at in range(0, rows, both):
        high, low = split(s_ref[at : at + both])
        keep[0, at : at + both] = high
        keep[1, at : at + both] = low
    plain[...] = mix(w_ref, 0, keep[0], keep[1])
    for k in range(size.batch):
        at = k * both
        plus, minus = plain[at : at + half], plain[at + half : at + both]
        add, sub = plus + minus, plus - minus
        data = jnp.concatenate(
            [
                side_by_side(add[:, :LANES], -add[:, LANES:]),
                side_by_side(sub[:, LANES:], sub[:, :LANES]),
            ],
            axis=0,
        )
        out = four_product(f_ref, data)
        for q in range(2):
            v_ref[q, k] = out[:, q * LANES : (q + 1) * LANES]


def lon_back_kernel(size, width, v_hbm, t_ref, out_ref, v_ref, sem):
    cols, slots = size.cols, size.slots
    step = pl.program_id(0)
    stride = size.row_slots
    flat = out_ref.reshape(size.band * cols, width)

    @pl.when(step == 0)
    def _():
        copies = []
        for q in range(2):
            tail = slots - size.freqs
            if tail:
                v_ref[pl.ds((q * slots + size.freqs) * stride, tail * stride), :] = jnp.zeros((tail * stride, LANES), F32)
            copies.append(
                pltpu.make_async_copy(
                    v_hbm.at[q], v_ref.at[pl.ds(q * slots * stride, size.freqs * stride), :], sem.at[q]
                )
            )
            copies[-1].start()
        for copy in copies:
            copy.wait()

    for pair in range(size.band // 2):
        data = side_by_side(
            *(
                v_ref[pl.ds(step * size.band + 2 * pair + i, 2 * slots, stride=stride), :]
                for i in range(2)
            )
        )
        high, low = split(data)
        out = three_product(t_ref, high, low)
        for i in range(2):
            at = (2 * pair + i) * cols
            flat[at : at + cols, :] = out[:cols, i * LANES : i * LANES + width]


def whole_spec(array):
    zeros = (0,) * array.ndim
    return pl.BlockSpec(array.shape, lambda *_: zeros)


def spectral_gradients(size, width, fields, weights, biases):
    tables = [stacked(lon_table(size, which)) for which in (False, True)]
    tables += [four_way(lat_table(size, which)) for which in (False, True)]
    consts = [jnp.asarray(table) for table in tables] + [weights, biases]
    bands, batches = size.rows // size.band, size.freqs // size.batch
    rows = size.batch * size.both
    field = pl.BlockSpec((size.band * size.cols // SUB, SUB, width), lambda i: (jnp.minimum(i, bands - 1), 0, 0))
    return pl.pallas_call(
        functools.partial(gradient_kernel, size, width, bands, batches),
        grid=(bands + batches,),
        in_specs=[field, field] + [whole_spec(const) for const in consts],
        out_specs=[
            pl.BlockSpec((rows, 2 * LANES), lambda i: (jnp.maximum(i - bands, 0), 0)),
            pl.BlockSpec((2, 2, width + SUB, LANES), lambda i: (0, 0, 0, 0)),
        ],
        out_shape=[
            jax.ShapeDtypeStruct((size.freqs * size.both, 2 * LANES), F32),
            jax.ShapeDtypeStruct((2, 2, width + SUB, LANES), F32),
        ],
        scratch_shapes=[
            pltpu.VMEM((size.band, 2, size.col_slots, 2 * LANES), BF16),
            pltpu.VMEM((2, size.row_slots * 2 * size.slots, LANES), F32),
            pltpu.VMEM((4, 2, rows, 2 * LANES), BF16),
            pltpu.VMEM((3, rows, 2 * LANES), F32),
            pltpu.VMEM((2, 2 * LANES, 2 * LANES), F32),
            pltpu.VMEM((2, SUB, 2 * LANES), F32),
        ],
        compiler_params=pltpu.CompilerParams(vmem_limit_bytes=VMEM_LIMIT),
        name="spectral_gradients",
    )(*fields, *consts)


def lat_back(size, s_modes, weights):
    lat = lat_table(size, False).T.copy()
    lat[:, size.half :] *= -1.0
    consts = [weights, jnp.asarray(four_way(lat))]
    rows = size.batch * size.both
    return pl.pallas_call(
        functools.partial(lat_back_kernel, size),
        grid=(size.freqs // size.batch,),
        in_specs=[pl.BlockSpec((rows, 2 * LANES), lambda i: (i, 0))] + [whole_spec(const) for const in consts],
        out_specs=pl.BlockSpec((2, size.batch, size.row_slots, LANES), lambda i: (0, i, 0, 0)),
        out_shape=jax.ShapeDtypeStruct((2, size.freqs, size.row_slots, LANES), F32),
        scratch_shapes=[
            pltpu.VMEM((2, rows, 2 * LANES), BF16),
            pltpu.VMEM((rows, 2 * LANES), F32),
        ],
        compiler_params=pltpu.CompilerParams(vmem_limit_bytes=VMEM_LIMIT),
        name="lat_back",
    )(s_modes, *consts)


def lon_back(size, width, v_modes):
    lon = lon_table(size, False).T
    table = jnp.asarray(stacked(lon))
    flat = v_modes.reshape(2, size.freqs * size.row_slots, LANES)
    return pl.pallas_call(
        functools.partial(lon_back_kernel, size, width),
        grid=(size.rows // size.band,),
        in_specs=[pl.BlockSpec(memory_space=pl.ANY), whole_spec(table)],
        out_specs=pl.BlockSpec((size.band * size.cols // SUB, SUB, width), lambda i: (i, 0, 0)),
        out_shape=jax.ShapeDtypeStruct((size.rows * size.cols // SUB, SUB, width), F32),
        scratch_shapes=[
            pltpu.VMEM((2 * size.slots * size.row_slots, LANES), F32),
            pltpu.SemaphoreType.DMA((2,)),
        ],
        compiler_params=pltpu.CompilerParams(vmem_limit_bytes=VMEM_LIMIT),
        name="lon_back",
    )(flat, table)


def mix_matrices(first, second):
    def matrix(weight):
        pad = LANES - weight.shape[-1]
        real, imag = (jnp.pad(part, ((0, pad), (0, pad))) for part in (weight[0], weight[1]))
        return jnp.concatenate([side_by_side(real, imag), side_by_side(-imag, real)], 0)

    one, two = matrix(first), matrix(second)
    every = jnp.stack([one, two, two.T, one.T])
    high = lax.reduce_precision(every, 8, 7)
    return jnp.stack([high, every - high], axis=1).astype(BF16)


def bias_rows(first, second):
    pad = LANES - first.shape[-1]
    return jnp.stack([jnp.pad(part, ((0, 0), (0, pad))).reshape(1, 2 * LANES) for part in (first, second)])


def sum_over_lat(value):
    count = lax.axis_size("lat")
    if count != 4:
        return lax.psum(value, "lat")
    one, two, three = (
        lax.ppermute(value, "lat", [(i, (i + s) % count) for i in range(count)]) for s in (1, 2, 3)
    )
    return (value + two) + (one + three)


def gather_over_lon(value):
    count = lax.axis_size("lon")
    me = lax.axis_index("lon")
    parts = [value] + [lax.ppermute(value, "lon", [(i, i ^ s) for i in range(count)]) for s in range(1, count)]
    return parts, me


def whole_block(layer_input, grad_output, first_weight, first_bias, second_weight, second_bias):
    _, width, lat_rows, lon_cols = layer_input.shape
    size = Sizes(lat_rows, lon_cols)
    block = lax.axis_index("lon")

    def mine(weight):
        return lax.dynamic_index_in_dim(weight, block, axis=1, keepdims=False)

    fields = [
        jnp.transpose(field, (0, 2, 3, 1)).reshape(-1, SUB, width)
        for field in (layer_input, grad_output)
    ]
    weights = mix_matrices(mine(first_weight), mine(second_weight))
    s_modes, partial = spectral_gradients(
        size, width, fields, weights[:3], bias_rows(mine(first_bias), mine(second_bias))
    )
    summed = sum_over_lat(partial)
    v_modes = lat_back(size, s_modes, weights[3:])
    summed, v_modes = lax.optimization_barrier((summed, v_modes))
    parts, me = gather_over_lon(summed)
    out = lon_back(size, width, v_modes)
    grad_input = out.reshape(lat_rows * lon_cols, width).T.reshape(1, width, lat_rows, lon_cols)
    stack = jnp.stack(parts)
    whole = jnp.stack(
        [lax.dynamic_index_in_dim(stack, me ^ b, 0, keepdims=False) for b in range(len(parts))], axis=2
    )
    weight_grads = whole[:, :, :, :width, :width]
    bias_grads = whole[:, :, :, width, :width]
    return (grad_input, weight_grads[0], bias_grads[0], weight_grads[1], bias_grads[1])


def tables(length, count, limit):
    first = jnp.arange(length, dtype=jnp.int32)[:, None]
    second = jnp.arange(count, dtype=jnp.int32)[None, :]
    angle = 2.0 * math.pi / length * (first * second % length).astype(jnp.float32)
    keeper = (second < limit).astype(jnp.float32) / math.sqrt(length)
    return (jnp.cos(angle) * keeper, jnp.sin(angle) * keeper)


def cotangent_weight(length, count):
    index = jnp.arange(count, dtype=jnp.int32)
    edge = (index == 0) | (2 * index == length)
    return jnp.where(edge, 1.0, 2.0).astype(jnp.float32)


def gelu_slope(value):
    inner = GELU_SCALE * (value + GELU_CUBE * value * value * value)
    tangent = jnp.tanh(inner)
    return 0.5 * (1.0 + tangent) + 0.5 * value * (1.0 - tangent * tangent) * GELU_SCALE * (
        1.0 + 3.0 * GELU_CUBE * value * value
    )


def complex_matrix(weight):
    real_part = weight[0]
    imag_part = weight[1]
    upper = jnp.stack([real_part, imag_part], axis=1)
    lower = jnp.stack([-imag_part, real_part], axis=1)
    return jnp.stack([upper, lower], axis=0)


def forward_mix(left, matrix):
    return jnp.einsum("psir,piqj->qsjr", left, matrix, precision=PRECISION)


def back_mix(left, matrix):
    return jnp.einsum("qsjr,piqj->psir", left, matrix, precision=PRECISION)


def weight_grad(left, right):
    total = jnp.einsum("psir,qsjr->piqj", left, right, precision=PRECISION)
    return jnp.stack(
        [total[0, :, 0, :] + total[1, :, 1, :], total[0, :, 1, :] - total[1, :, 0, :]]
    )


def bias_view(vector):
    return vector[:, None, :, None]


def block_backward(x_both, g_both, first_weight, first_bias, second_weight, second_bias):
    first_matrix = complex_matrix(first_weight)
    second_matrix = complex_matrix(second_weight)
    a_both = forward_mix(x_both, first_matrix) + bias_view(first_bias)
    o_both = jax.nn.gelu(a_both, approximate=True)
    z_both = forward_mix(o_both, second_matrix) + bias_view(second_bias)
    e_both = g_both * jnp.tanh(z_both / SHRINK) ** 2
    grad_w_two = weight_grad(o_both, e_both)
    grad_b_two = jnp.sum(e_both, axis=(1, 3))
    s_both = back_mix(e_both, second_matrix) * gelu_slope(a_both)
    grad_w_one = weight_grad(x_both, s_both)
    grad_b_one = jnp.sum(s_both, axis=(1, 3))
    d_both = back_mix(s_both, first_matrix)
    return d_both, (grad_w_one, grad_b_one, grad_w_two, grad_b_two)


def spread_block(layer_input, grad_output, first_weight, first_bias, second_weight, second_bias):
    lon_count = lax.axis_size("lon")
    samples, local_ch, lat_rows, lon_cols = layer_input.shape
    blocks, width = first_weight.shape[1], first_weight.shape[2]
    group = width // local_ch
    groups = [list(range(at, at + group)) for at in range(0, lon_count, group)]
    block = lax.axis_index("lon") // group
    kept_freqs = lon_cols // 2 + 1
    freq_slots = -(-kept_freqs // group) * group
    lon_cos, lon_sin = tables(lon_cols, freq_slots, kept_freqs)
    factor_row = cotangent_weight(lon_cols, freq_slots)[None, :]
    lon_table = jnp.stack([lon_cos, -lon_sin], axis=1)
    cot_table = jnp.stack([lon_cos * factor_row, -lon_sin * factor_row], axis=1)
    lon_back = jnp.stack([lon_cos.T, -lon_sin.T])
    lat_cos, lat_sin = tables(lat_rows, lat_rows, lat_rows)
    lat_table = jnp.stack(
        [jnp.stack([lat_cos, -lat_sin], axis=1), jnp.stack([lat_sin, lat_cos], axis=1)]
    )
    lat_back = jnp.stack(
        [jnp.stack([lat_cos, lat_sin], axis=1), jnp.stack([-lat_sin, lat_cos], axis=1)]
    )

    def spectrum(data, table):
        half = jnp.einsum("schw,wqk->qsckh", data, table, precision=PRECISION)
        full = jnp.einsum("psckh,phqm->qsckm", half, lat_table, precision=PRECISION)
        return full.reshape((2, samples, local_ch, freq_slots * lat_rows))

    def share(data, split, concat):
        if group == 1:
            return data
        return lax.all_to_all(
            data, "lon", split_axis=split, concat_axis=concat, axis_index_groups=groups, tiled=True
        )

    x_modes = share(spectrum(layer_input, lon_table), 3, 2)
    g_modes = share(spectrum(grad_output, cot_table), 3, 2)

    def mine(weight):
        return lax.dynamic_index_in_dim(weight, block, axis=1, keepdims=False)

    d_modes, partial_grads = block_backward(
        x_modes, g_modes, mine(first_weight), mine(first_bias), mine(second_weight), mine(second_bias)
    )
    flat_grads = jnp.concatenate([piece.reshape(-1) for piece in partial_grads])
    summed = lax.psum(flat_grads, "lat")
    if group > 1:
        summed = lax.psum(summed, "lon", axis_index_groups=groups)
    whole = lax.all_gather(summed, "lon", axis=0, tiled=False)[::group]
    stacked = share(d_modes, 2, 3)
    shape_five = (2, samples, local_ch, freq_slots, lat_rows)
    grad_input = jnp.einsum(
        "qsckh,qkw->schw",
        jnp.einsum("psckm,pmqh->qsckh", stacked.reshape(shape_five), lat_back, precision=PRECISION),
        lon_back,
        precision=PRECISION,
    )
    results = []
    offset = 0
    for piece in partial_grads:
        part = whole[:, offset : offset + piece.size].reshape((blocks,) + piece.shape)
        results.append(jnp.moveaxis(part, 0, 1))
        offset = offset + piece.size
    grad_w_one, grad_b_one, grad_w_two, grad_b_two = results
    return (grad_input, grad_w_one, grad_b_one, grad_w_two, grad_b_two)


def on_device(layer_input, grad_output, first_weight, first_bias, second_weight, second_bias):
    samples, local_ch, lat_rows, lon_cols = layer_input.shape
    width = first_weight.shape[2]
    one_device = samples == 1 and local_ch == width <= LANES and width % SUB == 0
    run = whole_block if one_device and Sizes(lat_rows, lon_cols).fits() else spread_block
    return run(layer_input, grad_output, first_weight, first_bias, second_weight, second_bias)


def solution(mesh):
    placed = (P("lat", "lon", None, None), P("lat", "lon", None, None), P(), P(), P(), P())
    return jax.shard_map(
        on_device,
        mesh=mesh,
        in_specs=placed,
        out_specs=(P("lat", "lon", None, None), P(), P(), P(), P()),
        check_vma=False,
    )
```

```python
import functools
import math

import jax
import jax.numpy as jnp
import ml_dtypes
import numpy as np
from jax import lax
from jax.experimental import pallas as pl
from jax.experimental.pallas import tpu as pltpu
from jax.sharding import PartitionSpec as P

SHRINK = 0.01
GELU_SCALE = math.sqrt(2.0 / math.pi)
GELU_CUBE = 0.044715
PRECISION = lax.Precision.HIGH
LANES = 128
SUB = 8
F32 = jnp.float32
BF16 = jnp.bfloat16
CHUNK = 4


def round_up(value, unit):
    return -(-value // unit) * unit


def halves(table):
    high = table.astype(ml_dtypes.bfloat16)
    low = (table - high.astype(np.float64)).astype(ml_dtypes.bfloat16)
    return high, low


def split(value):
    high = value.astype(BF16)
    return high, (value - high.astype(F32)).astype(BF16)


def dot(left, right):
    return jnp.dot(left, right, preferred_element_type=F32)


def side_by_side(left, right):
    return jnp.concatenate([left, right], axis=1)


def trig(length, count):
    first = np.arange(count)[:, None]
    second = np.arange(length)[None, :]
    angle = 2.0 * np.pi / length * (first * second % length)
    return np.cos(angle) / math.sqrt(length), np.sin(angle) / math.sqrt(length)


class Sizes:
    def __init__(self, rows, cols):
        self.rows, self.cols = rows, cols
        self.pairs = rows // 2 + 1
        self.half = round_up(self.pairs, SUB)
        self.both = 2 * self.half
        self.freqs = cols // 2 + 1
        self.slots = round_up(self.freqs, 16)
        self.stride = round_up(2 * self.slots, 2 * SUB) + SUB
        self.row_slots = round_up(rows, 16)
        self.col_slots = round_up(cols, 16)
        self.band = max((n for n in range(2, 11, 2) if rows % n == 0 and n * cols % SUB == 0), default=0)
        self.batch = SUB

    def fits(self):
        return self.band > 0 and self.cols % 4 == 0


def lat_table(size, cotangent):
    cos, sin = trig(size.rows, size.pairs)
    if cotangent:
        own = np.array([2 * m % size.rows == 0 for m in range(size.pairs)])
        cos, sin = (part * np.where(own, 0.5, 1.0)[:, None] for part in (cos, sin))
    table = np.zeros((size.both, size.row_slots))
    table[: size.pairs, : size.rows] = cos
    table[size.half : size.half + size.pairs, : size.rows] = sin
    return table


def lon_table(size, cotangent):
    cos, sin = trig(size.cols, size.freqs)
    if cotangent:
        index = np.arange(size.freqs)
        factor = np.where((index == 0) | (2 * index == size.cols), 1.0, 2.0)[:, None]
        cos, sin = cos * factor, sin * factor
    table = np.zeros((2 * size.slots, size.col_slots))
    table[: size.freqs, : size.cols] = cos
    table[size.slots : size.slots + size.freqs, : size.cols] = sin
    return table


def four_way(table):
    high, low = halves(table)
    return np.concatenate([np.concatenate([high, high], 1), np.concatenate([low, low], 1)], 0)


def three_way(table):
    high, low = halves(table)
    return np.concatenate([high, low, high], 1)


def four_product(table_ref, data):
    two = dot(table_ref[...], jnp.concatenate(split(data), axis=0))
    count = two.shape[0] // 2
    return two[:count] + two[count:]


def three_product(table_ref, high, low):
    return dot(table_ref[...], jnp.concatenate([high, high, low], axis=0))


def mix(weight_ref, which, high, low):
    return dot(jnp.concatenate([high, low, high], axis=1), weight_ref[which])


def gradient_kernel(
    size, width, bands, batches, x_ref, g_ref, tx_ref, tg_ref, fx_ref, fg_ref, w_ref, b_ref,
    s_ref, grad_ref, fold, spectra, keep, plain, total, bias_total,
):
    step = pl.program_id(0)
    cols, slots, both, half = size.cols, size.slots, size.both, size.half
    stride = size.stride
    lines = 2 * slots
    rows = size.batch * both

    @pl.when(step == 0)
    def _():
        fold[...] = jnp.zeros_like(fold)
        total[...] = jnp.zeros_like(total)
        bias_total[...] = jnp.zeros_like(bias_total)
        for which in range(2):
            spectra[which, size.rows * stride :] = jnp.zeros(((size.row_slots - size.rows) * stride, LANES), F32)

    @pl.when(step < bands)
    def _():
        for which, (field, table) in enumerate(((x_ref, tx_ref), (g_ref, tg_ref))):
            data = field.reshape(size.band * cols, width)
            for pair in range(size.band // 2):
                slot = which * (size.band // 2) + pair
                for i in range(2):
                    at = (2 * pair + i) * cols
                    high, low = split(data[at : at + cols, :])
                    fold[slot, 0, :cols, i * LANES : i * LANES + width] = high
                    fold[slot, 1, :cols, i * LANES : i * LANES + width] = low
                out = three_product(table, fold[slot, 0], fold[slot, 1])
                for i in range(2):
                    base = pl.multiple_of((step * size.band + 2 * pair + i) * stride, SUB)
                    spectra[which, pl.ds(base, lines), :] = out[:, i * LANES : (i + 1) * LANES]

    @pl.when(step >= bands)
    def _():
        first = (step - bands) * size.batch
        span = CHUNK * both
        piece = 16

        def transform(chunk):
            for k in range(chunk * CHUNK, (chunk + 1) * CHUNK):
                at = k * both
                for which, table in enumerate((fx_ref, fg_ref)):
                    data = side_by_side(
                        spectra[which, pl.ds(first + k, size.row_slots, stride=stride), :],
                        spectra[which, pl.ds(first + k + slots, size.row_slots, stride=stride), :],
                    )
                    out = four_product(table, data)
                    cos_one, cos_two = out[:half, :LANES], out[:half, LANES:]
                    sin_one, sin_two = out[half:, :LANES], out[half:, LANES:]
                    plus = side_by_side(cos_one - sin_two, -(cos_two + sin_one))
                    minus = side_by_side(cos_one + sin_two, sin_one - cos_two)
                    for part, value in ((0, plus), (1, minus)):
                        here = slice(at + part * half, at + (part + 1) * half)
                        if which == 0:
                            keep_split(0, here, value)
                        else:
                            plain[0, here] = value

        def keep_split(which, here, value):
            high, low = split(value)
            keep[which, 0, here] = high
            keep[which, 1, here] = low

        def multiply(which, chunk):
            here = slice(chunk * span, (chunk + 1) * span)
            plain[1 + which, here] = mix(w_ref, which, keep[which, 0, here], keep[which, 1, here])

        def pieces(chunk):
            return [slice(at, at + piece) for at in range(chunk * span, (chunk + 1) * span, piece)]

        def activate(chunk):
            for here in pieces(chunk):
                a = plain[1, here] + b_ref[0]
                square = a * a
                tangent = jnp.tanh(a * (GELU_SCALE + (GELU_SCALE * GELU_CUBE) * square))
                part = 0.5 * a
                plain[1, here] = 0.5 + 0.5 * tangent + part * (1.0 - tangent * tangent) * (
                    GELU_SCALE + (3.0 * GELU_SCALE * GELU_CUBE) * square
                )
                keep_split(1, here, part + part * tangent)

        def gate(chunk):
            sums = jnp.zeros((SUB, 2 * LANES), F32)
            for here in pieces(chunk):
                tangent = jnp.tanh((plain[2, here] + b_ref[1]) * (1.0 / SHRINK))
                e = plain[0, here] * (tangent * tangent)
                for i in range(0, piece, SUB):
                    sums = sums + e[i : i + SUB]
                keep_split(2, here, e)
            bias_total[1] += sums

        def slope(chunk):
            sums = jnp.zeros((SUB, 2 * LANES), F32)
            for here in pieces(chunk):
                value = plain[3, here] * plain[1, here]
                s_ref[here] = value
                for i in range(0, piece, SUB):
                    sums = sums + value[i : i + SUB]
                keep_split(3, here, value)
            bias_total[0] += sums

        def turned(which):
            parts = [keep[which, i].T for i in range(2)]
            return [jnp.concatenate([part[:width], part[LANES : LANES + width]], axis=0) for part in parts]

        def weight_grad(layer, left, right):
            high, low = turned(left)
            total[layer] += dot(
                jnp.concatenate([high, low, high], axis=1),
                jnp.concatenate([keep[right, 0], keep[right, 0], keep[right, 1]], axis=0),
            )

        count = size.batch // CHUNK
        for t in range(count + 3):
            if t < count:
                transform(t)
                multiply(0, t)
            if 0 <= t - 1 < count:
                activate(t - 1)
                multiply(1, t - 1)
            if 0 <= t - 2 < count:
                gate(t - 2)
                multiply(2, t - 2)
            if 0 <= t - 3 < count:
                slope(t - 3)
        weight_grad(1, 1, 2)
        weight_grad(0, 0, 3)

    @pl.when(step == bands + batches - 1)
    def _():
        for layer in range(2):
            upper = total[layer, :width]
            lower = total[layer, width:]
            grad_ref[layer, 0, :width] = upper[:, :LANES] + lower[:, LANES:]
            grad_ref[layer, 1, :width] = upper[:, LANES:] - lower[:, :LANES]
            bias = jnp.broadcast_to(jnp.sum(bias_total[layer], axis=0, keepdims=True), (SUB, 2 * LANES))
            grad_ref[layer, 0, width:] = bias[:, :LANES]
            grad_ref[layer, 1, width:] = bias[:, LANES:]


def lat_back_kernel(size, s_ref, w_ref, f_ref, v_ref, plain):
    both, half = size.both, size.half
    span = CHUNK * both

    def multiply(chunk):
        here = slice(chunk * span, (chunk + 1) * span)
        plain[here] = mix(w_ref, 0, *split(s_ref[here]))

    def transform(chunk):
        for k in range(chunk * CHUNK, (chunk + 1) * CHUNK):
            at = k * both
            plus, minus = plain[at : at + half], plain[at + half : at + both]
            add, sub = plus + minus, plus - minus
            data = jnp.concatenate(
                [
                    side_by_side(add[:, :LANES], -add[:, LANES:]),
                    side_by_side(sub[:, LANES:], sub[:, :LANES]),
                ],
                axis=0,
            )
            out = four_product(f_ref, data)
            for q in range(2):
                v_ref[q, k] = out[:, q * LANES : (q + 1) * LANES]

    count = size.batch // CHUNK
    for t in range(count + 1):
        if t < count:
            multiply(t)
        if t > 0:
            transform(t - 1)


def lon_back_kernel(size, width, v_ref, t_ref, out_ref):
    cols = size.cols
    lines = 2 * size.slots
    flat = out_ref.reshape(SUB * cols, width)
    rows = v_ref.reshape(lines * SUB, LANES)
    for pair in range(SUB // 2):
        data = side_by_side(*(rows[pl.ds(2 * pair + i, lines, stride=SUB), :] for i in range(2)))
        out = three_product(t_ref, *split(data))
        for i in range(2):
            at = (2 * pair + i) * cols
            flat[at : at + cols, :] = out[:cols, i * LANES : i * LANES + width]


def whole_spec(array):
    zeros = (0,) * array.ndim
    return pl.BlockSpec(array.shape, lambda *_: zeros)


def spectral_gradients(size, width, fields, weights, biases):
    tables = [three_way(lon_table(size, which)) for which in (False, True)]
    tables += [four_way(lat_table(size, which)) for which in (False, True)]
    consts = [jnp.asarray(table) for table in tables] + [weights, biases]
    bands, batches = size.rows // size.band, size.slots // size.batch
    rows = size.batch * size.both
    field = pl.BlockSpec((size.band * size.cols // SUB, SUB, width), lambda i: (jnp.minimum(i, bands - 1), 0, 0))
    return pl.pallas_call(
        functools.partial(gradient_kernel, size, width, bands, batches),
        grid=(bands + batches,),
        in_specs=[field, field] + [whole_spec(const) for const in consts],
        out_specs=[
            pl.BlockSpec((rows, 2 * LANES), lambda i: (jnp.maximum(i - bands, 0), 0)),
            pl.BlockSpec((2, 2, width + SUB, LANES), lambda i: (0, 0, 0, 0)),
        ],
        out_shape=[
            jax.ShapeDtypeStruct((size.slots * size.both, 2 * LANES), F32),
            jax.ShapeDtypeStruct((2, 2, width + SUB, LANES), F32),
        ],
        scratch_shapes=[
            pltpu.VMEM((size.band, 2, size.col_slots, 2 * LANES), BF16),
            pltpu.VMEM((2, size.row_slots * size.stride, LANES), F32),
            pltpu.VMEM((4, 2, rows, 2 * LANES), BF16),
            pltpu.VMEM((4, rows, 2 * LANES), F32),
            pltpu.VMEM((2, 2 * width, 2 * LANES), F32),
            pltpu.VMEM((2, SUB, 2 * LANES), F32),
        ],
        compiler_params=pltpu.CompilerParams(vmem_limit_bytes=40 << 20),
        name="spectral_gradients",
    )(*fields, *consts)


def lat_back(size, s_modes, weights):
    lat = lat_table(size, False).T.copy()
    lat[:, size.half :] *= -1.0
    consts = [weights, jnp.asarray(four_way(lat))]
    rows = size.batch * size.both
    return pl.pallas_call(
        functools.partial(lat_back_kernel, size),
        grid=(size.slots // size.batch,),
        in_specs=[pl.BlockSpec((rows, 2 * LANES), lambda i: (i, 0))] + [whole_spec(const) for const in consts],
        out_specs=pl.BlockSpec((2, size.batch, size.row_slots, LANES), lambda i: (0, i, 0, 0)),
        out_shape=jax.ShapeDtypeStruct((2, size.slots, size.row_slots, LANES), F32),
        scratch_shapes=[pltpu.VMEM((rows, 2 * LANES), F32)],
        compiler_params=pltpu.CompilerParams(vmem_limit_bytes=12 << 20),
        name="lat_back",
    )(s_modes, *consts)


def lon_back(size, width, v_modes):
    lon = lon_table(size, False).T
    table = jnp.asarray(three_way(lon))
    return pl.pallas_call(
        functools.partial(lon_back_kernel, size, width),
        grid=(size.row_slots // SUB,),
        in_specs=[pl.BlockSpec((2, size.slots, SUB, LANES), lambda i: (0, 0, i, 0)), whole_spec(table)],
        out_specs=pl.BlockSpec((size.cols, SUB, width), lambda i: (i, 0, 0)),
        out_shape=jax.ShapeDtypeStruct((size.rows * size.cols // SUB, SUB, width), F32),
        compiler_params=pltpu.CompilerParams(vmem_limit_bytes=12 << 20),
        name="lon_back",
    )(v_modes, table)


def mix_matrices(first, second):
    def matrix(weight):
        pad = LANES - weight.shape[-1]
        real, imag = (jnp.pad(part, ((0, pad), (0, pad))) for part in (weight[0], weight[1]))
        return jnp.concatenate([side_by_side(real, imag), side_by_side(-imag, real)], 0)

    one, two = matrix(first), matrix(second)
    every = jnp.stack([one, two, two.T, one.T])
    high = lax.reduce_precision(every, 8, 7)
    return jnp.concatenate([high, high, every - high], axis=1).astype(BF16)


def bias_rows(first, second):
    pad = LANES - first.shape[-1]
    return jnp.stack([jnp.pad(part, ((0, 0), (0, pad))).reshape(1, 2 * LANES) for part in (first, second)])


def sum_over_lat(value):
    count = lax.axis_size("lat")
    if count != 4:
        return lax.psum(value, "lat")
    one, two, three = (
        lax.ppermute(value, "lat", [(i, (i + s) % count) for i in range(count)]) for s in (1, 2, 3)
    )
    return (value + two) + (one + three)


def gather_over_lon(value):
    count = lax.axis_size("lon")
    me = lax.axis_index("lon")
    parts = [value] + [lax.ppermute(value, "lon", [(i, i ^ s) for i in range(count)]) for s in range(1, count)]
    return parts, me


def whole_block(layer_input, grad_output, first_weight, first_bias, second_weight, second_bias):
    _, width, lat_rows, lon_cols = layer_input.shape
    size = Sizes(lat_rows, lon_cols)
    block = lax.axis_index("lon")

    def mine(weight):
        return lax.dynamic_index_in_dim(weight, block, axis=1, keepdims=False)

    fields = [
        jnp.transpose(field, (0, 2, 3, 1)).reshape(-1, SUB, width)
        for field in (layer_input, grad_output)
    ]
    weights = mix_matrices(mine(first_weight), mine(second_weight))
    s_modes, partial = spectral_gradients(
        size, width, fields, weights[:3], bias_rows(mine(first_bias), mine(second_bias))
    )
    summed = sum_over_lat(partial)
    v_modes = lat_back(size, s_modes, weights[3:])
    summed, v_modes = lax.optimization_barrier((summed, v_modes))
    parts, me = gather_over_lon(summed)
    out = lon_back(size, width, v_modes)
    grad_input = out.reshape(lat_rows * lon_cols, width).T.reshape(1, width, lat_rows, lon_cols)
    stack = jnp.stack(parts)
    whole = jnp.stack(
        [lax.dynamic_index_in_dim(stack, me ^ b, 0, keepdims=False) for b in range(len(parts))], axis=2
    )
    weight_grads = whole[:, :, :, :width, :width]
    bias_grads = whole[:, :, :, width, :width]
    return (grad_input, weight_grads[0], bias_grads[0], weight_grads[1], bias_grads[1])


def tables(length, count, limit):
    first = jnp.arange(length, dtype=jnp.int32)[:, None]
    second = jnp.arange(count, dtype=jnp.int32)[None, :]
    angle = 2.0 * math.pi / length * (first * second % length).astype(jnp.float32)
    keeper = (second < limit).astype(jnp.float32) / math.sqrt(length)
    return (jnp.cos(angle) * keeper, jnp.sin(angle) * keeper)


def cotangent_weight(length, count):
    index = jnp.arange(count, dtype=jnp.int32)
    edge = (index == 0) | (2 * index == length)
    return jnp.where(edge, 1.0, 2.0).astype(jnp.float32)


def gelu_slope(value):
    inner = GELU_SCALE * (value + GELU_CUBE * value * value * value)
    tangent = jnp.tanh(inner)
    return 0.5 * (1.0 + tangent) + 0.5 * value * (1.0 - tangent * tangent) * GELU_SCALE * (
        1.0 + 3.0 * GELU_CUBE * value * value
    )


def complex_matrix(weight):
    real_part = weight[0]
    imag_part = weight[1]
    upper = jnp.stack([real_part, imag_part], axis=1)
    lower = jnp.stack([-imag_part, real_part], axis=1)
    return jnp.stack([upper, lower], axis=0)


def forward_mix(left, matrix):
    return jnp.einsum("psir,piqj->qsjr", left, matrix, precision=PRECISION)


def back_mix(left, matrix):
    return jnp.einsum("qsjr,piqj->psir", left, matrix, precision=PRECISION)


def weight_grad(left, right):
    total = jnp.einsum("psir,qsjr->piqj", left, right, precision=PRECISION)
    return jnp.stack(
        [total[0, :, 0, :] + total[1, :, 1, :], total[0, :, 1, :] - total[1, :, 0, :]]
    )


def bias_view(vector):
    return vector[:, None, :, None]


def block_backward(x_both, g_both, first_weight, first_bias, second_weight, second_bias):
    first_matrix = complex_matrix(first_weight)
    second_matrix = complex_matrix(second_weight)
    a_both = forward_mix(x_both, first_matrix) + bias_view(first_bias)
    o_both = jax.nn.gelu(a_both, approximate=True)
    z_both = forward_mix(o_both, second_matrix) + bias_view(second_bias)
    e_both = g_both * jnp.tanh(z_both / SHRINK) ** 2
    grad_w_two = weight_grad(o_both, e_both)
    grad_b_two = jnp.sum(e_both, axis=(1, 3))
    s_both = back_mix(e_both, second_matrix) * gelu_slope(a_both)
    grad_w_one = weight_grad(x_both, s_both)
    grad_b_one = jnp.sum(s_both, axis=(1, 3))
    d_both = back_mix(s_both, first_matrix)
    return d_both, (grad_w_one, grad_b_one, grad_w_two, grad_b_two)


def spread_block(layer_input, grad_output, first_weight, first_bias, second_weight, second_bias):
    lon_count = lax.axis_size("lon")
    samples, local_ch, lat_rows, lon_cols = layer_input.shape
    blocks, width = first_weight.shape[1], first_weight.shape[2]
    group = width // local_ch
    groups = [list(range(at, at + group)) for at in range(0, lon_count, group)]
    block = lax.axis_index("lon") // group
    kept_freqs = lon_cols // 2 + 1
    freq_slots = -(-kept_freqs // group) * group
    lon_cos, lon_sin = tables(lon_cols, freq_slots, kept_freqs)
    factor_row = cotangent_weight(lon_cols, freq_slots)[None, :]
    lon_table = jnp.stack([lon_cos, -lon_sin], axis=1)
    cot_table = jnp.stack([lon_cos * factor_row, -lon_sin * factor_row], axis=1)
    lon_back = jnp.stack([lon_cos.T, -lon_sin.T])
    lat_cos, lat_sin = tables(lat_rows, lat_rows, lat_rows)
    lat_table = jnp.stack(
        [jnp.stack([lat_cos, -lat_sin], axis=1), jnp.stack([lat_sin, lat_cos], axis=1)]
    )
    lat_back = jnp.stack(
        [jnp.stack([lat_cos, lat_sin], axis=1), jnp.stack([-lat_sin, lat_cos], axis=1)]
    )

    def spectrum(data, table):
        half = jnp.einsum("schw,wqk->qsckh", data, table, precision=PRECISION)
        full = jnp.einsum("psckh,phqm->qsckm", half, lat_table, precision=PRECISION)
        return full.reshape((2, samples, local_ch, freq_slots * lat_rows))

    def share(data, split, concat):
        if group == 1:
            return data
        return lax.all_to_all(
            data, "lon", split_axis=split, concat_axis=concat, axis_index_groups=groups, tiled=True
        )

    x_modes = share(spectrum(layer_input, lon_table), 3, 2)
    g_modes = share(spectrum(grad_output, cot_table), 3, 2)

    def mine(weight):
        return lax.dynamic_index_in_dim(weight, block, axis=1, keepdims=False)

    d_modes, partial_grads = block_backward(
        x_modes, g_modes, mine(first_weight), mine(first_bias), mine(second_weight), mine(second_bias)
    )
    flat_grads = jnp.concatenate([piece.reshape(-1) for piece in partial_grads])
    summed = lax.psum(flat_grads, "lat")
    if group > 1:
        summed = lax.psum(summed, "lon", axis_index_groups=groups)
    whole = lax.all_gather(summed, "lon", axis=0, tiled=False)[::group]
    stacked = share(d_modes, 2, 3)
    shape_five = (2, samples, local_ch, freq_slots, lat_rows)
    grad_input = jnp.einsum(
        "qsckh,qkw->schw",
        jnp.einsum("psckm,pmqh->qsckh", stacked.reshape(shape_five), lat_back, precision=PRECISION),
        lon_back,
        precision=PRECISION,
    )
    results = []
    offset = 0
    for piece in partial_grads:
        part = whole[:, offset : offset + piece.size].reshape((blocks,) + piece.shape)
        results.append(jnp.moveaxis(part, 0, 1))
        offset = offset + piece.size
    grad_w_one, grad_b_one, grad_w_two, grad_b_two = results
    return (grad_input, grad_w_one, grad_b_one, grad_w_two, grad_b_two)


def on_device(layer_input, grad_output, first_weight, first_bias, second_weight, second_bias):
    samples, local_ch, lat_rows, lon_cols = layer_input.shape
    width = first_weight.shape[2]
    one_device = samples == 1 and local_ch == width <= LANES and width % SUB == 0
    run = whole_block if one_device and Sizes(lat_rows, lon_cols).fits() else spread_block
    return run(layer_input, grad_output, first_weight, first_bias, second_weight, second_bias)


def solution(mesh):
    placed = (P("lat", "lon", None, None), P("lat", "lon", None, None), P(), P(), P(), P())
    return jax.shard_map(
        on_device,
        mesh=mesh,
        in_specs=placed,
        out_specs=(P("lat", "lon", None, None), P(), P(), P(), P()),
        check_vma=False,
    )
```

```python
import functools
import math

import jax
import jax.numpy as jnp
import ml_dtypes
import numpy as np
from jax import lax
from jax.experimental import pallas as pl
from jax.experimental.pallas import tpu as pltpu
from jax.sharding import PartitionSpec as P

SHRINK = 0.01
GELU_SCALE = math.sqrt(2.0 / math.pi)
GELU_CUBE = 0.044715
PRECISION = lax.Precision.HIGH
LANES = 128
SUB = 8
F32 = jnp.float32
BF16 = jnp.bfloat16
CHUNK = 4
BAND_MOST = 10
PARTS = 2
GRADIENT_VMEM = 54 << 20
LAT_VMEM = 24 << 20
LON_VMEM = 24 << 20


def round_up(value, unit):
    return -(-value // unit) * unit


def halves(table):
    high = table.astype(ml_dtypes.bfloat16)
    low = (table - high.astype(np.float64)).astype(ml_dtypes.bfloat16)
    return high, low


def split(value):
    high = value.astype(BF16)
    return high, (value - high.astype(F32)).astype(BF16)


def dot(left, right):
    return jnp.dot(left, right, preferred_element_type=F32)


def side_by_side(left, right):
    return jnp.concatenate([left, right], axis=1)


def trig(length, count):
    first = np.arange(count)[:, None]
    second = np.arange(length)[None, :]
    angle = 2.0 * np.pi / length * (first * second % length)
    return np.cos(angle) / math.sqrt(length), np.sin(angle) / math.sqrt(length)


class Sizes:
    def __init__(self, rows, cols):
        self.rows, self.cols = rows, cols
        self.pairs = rows // 2 + 1
        self.half = round_up(self.pairs, SUB)
        self.both = 2 * self.half
        self.freqs = cols // 2 + 1
        self.slots = round_up(self.freqs, 16)
        self.stride = round_up(2 * self.slots, 2 * SUB) + SUB
        self.row_slots = round_up(rows, 16)
        self.col_slots = round_up(cols, 16)
        self.band = max((n for n in range(2, BAND_MOST + 1, 2) if rows % n == 0 and n * cols % SUB == 0), default=0)
        self.batch = SUB

    def fits(self):
        return self.band > 0 and self.cols % 4 == 0


def lat_table(size, cotangent):
    cos, sin = trig(size.rows, size.pairs)
    if cotangent:
        own = np.array([2 * m % size.rows == 0 for m in range(size.pairs)])
        cos, sin = (part * np.where(own, 0.5, 1.0)[:, None] for part in (cos, sin))
    table = np.zeros((size.both, size.row_slots))
    table[: size.pairs, : size.rows] = cos
    table[size.half : size.half + size.pairs, : size.rows] = sin
    return table


def lon_table(size, cotangent):
    cos, sin = trig(size.cols, size.freqs)
    if cotangent:
        index = np.arange(size.freqs)
        factor = np.where((index == 0) | (2 * index == size.cols), 1.0, 2.0)[:, None]
        cos, sin = cos * factor, sin * factor
    table = np.zeros((2 * size.slots, size.col_slots))
    table[: size.freqs, : size.cols] = cos
    table[size.slots : size.slots + size.freqs, : size.cols] = sin
    return table


def four_way(table):
    high, low = halves(table)
    return np.concatenate([np.concatenate([high, high], 1), np.concatenate([low, low], 1)], 0)


def three_way(table):
    high, low = halves(table)
    return np.concatenate([high, low, high], 1)


def four_product(table_ref, data):
    two = dot(table_ref[...], jnp.concatenate(split(data), axis=0))
    count = two.shape[0] // 2
    return two[:count] + two[count:]


def three_product(table_ref, high, low):
    return dot(table_ref[...], jnp.concatenate([high, high, low], axis=0))


def mix(weight_ref, which, high, low):
    return dot(jnp.concatenate([high, low, high], axis=1), weight_ref[which])


def fill_matrix(out, width, real, imag, turned):
    if turned:
        real, imag = real.T, imag.T
    sign = -1.0 if turned else 1.0
    span = 2 * LANES
    for row, column, value in ((0, 0, real), (1, 1, real), (0, 1, sign * imag), (1, 0, -sign * imag)):
        high, low = split(value)
        columns = slice(column * LANES, column * LANES + width)
        for third, part in enumerate((high, high, low)):
            at = third * span + row * LANES
            out[at : at + width, columns] = part


def gradient_kernel(
    size, width, bands, batches, at_ref, x_ref, g_ref, tx_ref, tg_ref, fx_ref, fg_ref, wa_ref, wb_ref, ba_ref, bb_ref,
    s_ref, grad_ref, fold, spectra, keep, plain, total, bias_total, w_ref, b_ref,
):
    step = pl.program_id(0)
    cols, slots, both, half = size.cols, size.slots, size.both, size.half
    stride = size.stride
    lines = 2 * slots
    rows = size.batch * both

    @pl.when(step == 0)
    def _():
        fold[...] = jnp.zeros_like(fold)
        total[...] = jnp.zeros_like(total)
        bias_total[...] = jnp.zeros_like(bias_total)
        w_ref[...] = jnp.zeros_like(w_ref)
        b_ref[...] = jnp.zeros_like(b_ref)
        fill_matrix(w_ref.at[0], width, wa_ref[0, 0], wa_ref[1, 0], False)
        fill_matrix(w_ref.at[1], width, wb_ref[0, 0], wb_ref[1, 0], False)
        fill_matrix(w_ref.at[2], width, wb_ref[0, 0], wb_ref[1, 0], True)
        for layer, bias in enumerate((ba_ref, bb_ref)):
            for q in range(2):
                row = bias[q, pl.ds(at_ref[1], 1), :]
                b_ref[layer, :, q * LANES : q * LANES + width] = jnp.broadcast_to(row, (SUB, width))
        for which in range(2):
            spectra[which, size.rows * stride :] = jnp.zeros(((size.row_slots - size.rows) * stride, LANES), F32)

    @pl.when(step < bands)
    def _():
        for which, (field, table) in enumerate(((x_ref, tx_ref), (g_ref, tg_ref))):
            data = field.reshape(size.band * cols, width)
            for pair in range(size.band // 2):
                slot = which * (size.band // 2) + pair
                for i in range(2):
                    at = (2 * pair + i) * cols
                    high, low = split(data[at : at + cols, :])
                    fold[slot, 0, :cols, i * LANES : i * LANES + width] = high
                    fold[slot, 1, :cols, i * LANES : i * LANES + width] = low
                out = three_product(table, fold[slot, 0], fold[slot, 1])
                for i in range(2):
                    base = pl.multiple_of((step * size.band + 2 * pair + i) * stride, SUB)
                    spectra[which, pl.ds(base, lines), :] = out[:, i * LANES : (i + 1) * LANES]

    @pl.when(step >= bands)
    def _():
        first = (step - bands) * size.batch
        span = CHUNK * both
        piece = 16

        def transform(chunk):
            for k in range(chunk * CHUNK, (chunk + 1) * CHUNK):
                at = k * both
                for which, table in enumerate((fx_ref, fg_ref)):
                    data = side_by_side(
                        spectra[which, pl.ds(first + k, size.row_slots, stride=stride), :],
                        spectra[which, pl.ds(first + k + slots, size.row_slots, stride=stride), :],
                    )
                    out = four_product(table, data)
                    cos_one, cos_two = out[:half, :LANES], out[:half, LANES:]
                    sin_one, sin_two = out[half:, :LANES], out[half:, LANES:]
                    plus = side_by_side(cos_one - sin_two, -(cos_two + sin_one))
                    minus = side_by_side(cos_one + sin_two, sin_one - cos_two)
                    for part, value in ((0, plus), (1, minus)):
                        here = slice(at + part * half, at + (part + 1) * half)
                        if which == 0:
                            keep_split(0, here, value)
                        else:
                            plain[0, here] = value

        def keep_split(which, here, value):
            high, low = split(value)
            keep[which, 0, here] = high
            keep[which, 1, here] = low

        def multiply(which, chunk):
            here = slice(chunk * span, (chunk + 1) * span)
            plain[1 + which, here] = mix(w_ref, which, keep[which, 0, here], keep[which, 1, here])

        def pieces(chunk):
            return [slice(at, at + piece) for at in range(chunk * span, (chunk + 1) * span, piece)]

        def activate(chunk):
            for here in pieces(chunk):
                a = plain[1, here] + b_ref[0, :1]
                square = a * a
                tangent = jnp.tanh(a * (GELU_SCALE + (GELU_SCALE * GELU_CUBE) * square))
                part = 0.5 * a
                plain[1, here] = 0.5 + 0.5 * tangent + part * (1.0 - tangent * tangent) * (
                    GELU_SCALE + (3.0 * GELU_SCALE * GELU_CUBE) * square
                )
                keep_split(1, here, part + part * tangent)

        def gate(chunk):
            sums = jnp.zeros((SUB, 2 * LANES), F32)
            for here in pieces(chunk):
                tangent = jnp.tanh((plain[2, here] + b_ref[1, :1]) * (1.0 / SHRINK))
                e = plain[0, here] * (tangent * tangent)
                for i in range(0, piece, SUB):
                    sums = sums + e[i : i + SUB]
                keep_split(2, here, e)
            bias_total[1] += sums

        def slope(chunk):
            sums = jnp.zeros((SUB, 2 * LANES), F32)
            for here in pieces(chunk):
                value = plain[3, here] * plain[1, here]
                s_ref[here] = value
                for i in range(0, piece, SUB):
                    sums = sums + value[i : i + SUB]
                keep_split(3, here, value)
            bias_total[0] += sums

        def turned(which):
            parts = [keep[which, i].T for i in range(2)]
            return [jnp.concatenate([part[:width], part[LANES : LANES + width]], axis=0) for part in parts]

        def weight_grad(layer, left, right):
            high, low = turned(left)
            total[layer] += dot(
                jnp.concatenate([high, low, high], axis=1),
                jnp.concatenate([keep[right, 0], keep[right, 0], keep[right, 1]], axis=0),
            )

        count = size.batch // CHUNK
        for t in range(count + 3):
            if t < count:
                transform(t)
                multiply(0, t)
            if 0 <= t - 1 < count:
                activate(t - 1)
                multiply(1, t - 1)
            if 0 <= t - 2 < count:
                gate(t - 2)
                multiply(2, t - 2)
            if 0 <= t - 3 < count:
                slope(t - 3)
        weight_grad(1, 1, 2)
        weight_grad(0, 0, 3)

    @pl.when(step == bands + batches - 1)
    def _():
        for layer in range(2):
            upper = total[layer, :width]
            lower = total[layer, width:]
            grad_ref[layer, 0, :width] = upper[:, :LANES] + lower[:, LANES:]
            grad_ref[layer, 1, :width] = upper[:, LANES:] - lower[:, :LANES]
            bias = jnp.broadcast_to(jnp.sum(bias_total[layer], axis=0, keepdims=True), (SUB, 2 * LANES))
            grad_ref[layer, 0, width:] = bias[:, :LANES]
            grad_ref[layer, 1, width:] = bias[:, LANES:]


def lat_back_kernel(size, width, at_ref, s_ref, wa_ref, f_ref, v_ref, plain, w_ref):
    both, half = size.both, size.half
    span = CHUNK * both

    @pl.when(pl.program_id(0) == 0)
    def _():
        w_ref[...] = jnp.zeros_like(w_ref)
        fill_matrix(w_ref.at[0], width, wa_ref[0, 0], wa_ref[1, 0], True)

    def multiply(chunk):
        here = slice(chunk * span, (chunk + 1) * span)
        plain[here] = mix(w_ref, 0, *split(s_ref[here]))

    def transform(chunk):
        for k in range(chunk * CHUNK, (chunk + 1) * CHUNK):
            at = k * both
            plus, minus = plain[at : at + half], plain[at + half : at + both]
            add, sub = plus + minus, plus - minus
            data = jnp.concatenate(
                [
                    side_by_side(add[:, :LANES], -add[:, LANES:]),
                    side_by_side(sub[:, LANES:], sub[:, :LANES]),
                ],
                axis=0,
            )
            out = four_product(f_ref, data)
            for q in range(2):
                v_ref[q, k] = out[:, q * LANES : (q + 1) * LANES]

    count = size.batch // CHUNK
    for t in range(count + 1):
        if t < count:
            multiply(t)
        if t > 0:
            transform(t - 1)


def lon_back_kernel(size, width, *refs):
    v_refs, (t_ref, out_ref) = refs[:PARTS], refs[PARTS:]
    cols = size.cols
    lines = size.slots // PARTS
    flat = out_ref.reshape(SUB * cols, width)
    rows = [ref.reshape(2 * lines * SUB, LANES) for ref in v_refs]
    for pair in range(SUB // 2):
        data = side_by_side(
            *(
                jnp.concatenate(
                    [
                        part[pl.ds(q * lines * SUB + 2 * pair + i, lines, stride=SUB), :]
                        for q in range(2)
                        for part in rows
                    ],
                    axis=0,
                )
                for i in range(2)
            )
        )
        out = three_product(t_ref, *split(data))
        for i in range(2):
            at = (2 * pair + i) * cols
            flat[at : at + cols, :] = out[:cols, i * LANES : i * LANES + width]


def assemble_kernel(width, count, at_ref, *refs):
    parts, (wa_ref, wb_ref, ba_ref, bb_ref) = refs[:count], refs[count:]
    for l, (weight, bias) in enumerate(((wa_ref, ba_ref), (wa_ref, ba_ref), (wb_ref, bb_ref), (wb_ref, bb_ref))):
        shift = lax.rem(at_ref[0] + 4 - l, 4)
        for x in range(count):
            block = at_ref[2 + x]
            weight[l % 2, block] = parts[x][shift, :width, :width]
            bias[l % 2, pl.ds(block, 1), :] = parts[x][shift, width : width + 1, :width]


def whole_spec(array):
    zeros = (0,) * array.ndim
    return pl.BlockSpec(array.shape, lambda *_: zeros)


def spectral_gradients(size, place, fields, first_weight, first_bias, second_weight, second_bias):
    width = first_weight.shape[-1]
    tables = [three_way(lon_table(size, which)) for which in (False, True)]
    tables += [four_way(lat_table(size, which)) for which in (False, True)]
    consts = [jnp.asarray(table) for table in tables]
    weight = pl.BlockSpec((2, 1, width, width), lambda i, at: (0, at[1], 0, 0))
    bias = whole_spec(first_bias)
    bands, batches = size.rows // size.band, size.slots // size.batch
    rows = size.batch * size.both
    field = pl.BlockSpec((size.band * size.cols // SUB, SUB, width), lambda i, at: (jnp.minimum(i, bands - 1), 0, 0))
    return pl.pallas_call(
        functools.partial(gradient_kernel, size, width, bands, batches),
        grid_spec=pltpu.PrefetchScalarGridSpec(
            num_scalar_prefetch=1,
            grid=(bands + batches,),
            in_specs=[field, field] + [whole_spec(const) for const in consts] + [weight, weight, bias, bias],
            out_specs=[
                pl.BlockSpec((rows, 2 * LANES), lambda i, at: (jnp.maximum(i - bands, 0), 0)),
                pl.BlockSpec((2, 2, width + SUB, LANES), lambda i, at: (0, 0, 0, 0)),
            ],
            scratch_shapes=[
                pltpu.VMEM((size.band, 2, size.col_slots, 2 * LANES), BF16),
                pltpu.VMEM((2, size.row_slots * size.stride, LANES), F32),
                pltpu.VMEM((4, 2, rows, 2 * LANES), BF16),
                pltpu.VMEM((4, rows, 2 * LANES), F32),
                pltpu.VMEM((2, 2 * width, 2 * LANES), F32),
                pltpu.VMEM((2, SUB, 2 * LANES), F32),
                pltpu.VMEM((3, 6 * LANES, 2 * LANES), BF16),
                pltpu.VMEM((2, SUB, 2 * LANES), F32),
            ],
        ),
        out_shape=[
            jax.ShapeDtypeStruct((size.slots * size.both, 2 * LANES), F32),
            jax.ShapeDtypeStruct((2, 2, width + SUB, LANES), F32),
        ],
        compiler_params=pltpu.CompilerParams(vmem_limit_bytes=GRADIENT_VMEM),
        name="spectral_gradients",
    )(place, *fields, *consts, first_weight, second_weight, first_bias, second_bias)


def lat_back(size, place, s_modes, weight, part):
    width = weight.shape[-1]
    lat = lat_table(size, False).T.copy()
    lat[:, size.half :] *= -1.0
    table = jnp.asarray(four_way(lat))
    rows = size.batch * size.both
    steps = size.slots // size.batch // PARTS
    return pl.pallas_call(
        functools.partial(lat_back_kernel, size, width),
        grid_spec=pltpu.PrefetchScalarGridSpec(
            num_scalar_prefetch=1,
            grid=(steps,),
            in_specs=[
                pl.BlockSpec((rows, 2 * LANES), lambda i, at: (part * steps + i, 0)),
                pl.BlockSpec((2, 1, width, width), lambda i, at: (0, at[1], 0, 0)),
                whole_spec(table),
            ],
            out_specs=pl.BlockSpec((2, size.batch, size.row_slots, LANES), lambda i, at: (0, i, 0, 0)),
            scratch_shapes=[pltpu.VMEM((rows, 2 * LANES), F32), pltpu.VMEM((1, 6 * LANES, 2 * LANES), BF16)],
        ),
        out_shape=jax.ShapeDtypeStruct((2, size.slots // PARTS, size.row_slots, LANES), F32),
        compiler_params=pltpu.CompilerParams(vmem_limit_bytes=LAT_VMEM),
        name="lat_back",
    )(place, s_modes, weight, table)


def lon_back(size, width, v_parts):
    table = jnp.asarray(three_way(lon_table(size, False).T))
    field = pl.BlockSpec((2, size.slots // PARTS, SUB, LANES), lambda i: (0, 0, i, 0))
    return pl.pallas_call(
        functools.partial(lon_back_kernel, size, width),
        grid=(size.row_slots // SUB,),
        in_specs=[field] * PARTS + [whole_spec(table)],
        out_specs=pl.BlockSpec((size.cols, SUB, width), lambda i: (i, 0, 0)),
        out_shape=jax.ShapeDtypeStruct((size.rows * size.cols // SUB, SUB, width), F32),
        compiler_params=pltpu.CompilerParams(vmem_limit_bytes=LON_VMEM),
        name="lon_back",
    )(*v_parts, table)


def assemble(place, parts, width):
    count = len(parts)
    shapes = [(2, count, width, width)] * 2 + [(2, count, width)] * 2
    memory = pl.BlockSpec(memory_space=pltpu.VMEM)
    return pl.pallas_call(
        functools.partial(assemble_kernel, width, count),
        in_specs=[pl.BlockSpec(memory_space=pltpu.SMEM)] + [memory] * count,
        out_specs=[memory] * 4,
        out_shape=[jax.ShapeDtypeStruct(shape, F32) for shape in shapes],
        compiler_params=pltpu.CompilerParams(vmem_limit_bytes=LON_VMEM),
        name="assemble",
    )(place, *parts)


def shifted(value, axis, shift):
    count = lax.axis_size(axis)
    return lax.ppermute(value, axis, [(i, (i + shift) % count) for i in range(count)])


def crossed(value, axis, mask):
    count = lax.axis_size(axis)
    return lax.ppermute(value, axis, [(i, i ^ mask) for i in range(count)])


def whole_block(layer_input, grad_output, first_weight, first_bias, second_weight, second_bias):
    _, width, lat_rows, lon_cols = layer_input.shape
    size = Sizes(lat_rows, lon_cols)
    at_lat, at_lon = lax.axis_index("lat"), lax.axis_index("lon")
    place = jnp.stack([at_lat, at_lon] + [at_lon ^ x for x in range(lax.axis_size("lon"))])
    fields = [
        jnp.transpose(field, (0, 2, 3, 1)).reshape(-1, SUB, width) for field in (layer_input, grad_output)
    ]
    s_modes, partial = spectral_gradients(
        size, place, fields, first_weight, first_bias, second_weight, second_bias
    )
    matrices = partial.reshape(4, width + SUB, LANES)

    def matrix(shift):
        return lax.dynamic_index_in_dim(matrices, (at_lat + shift) % 4, 0, keepdims=False)

    far = [shifted(matrix(shift), "lat", shift) for shift in (1, 2, 3)]
    v_first = lat_back(size, place, s_modes, first_weight, 0)
    far, v_first, s_modes = lax.optimization_barrier((far, v_first, s_modes))
    mine = (matrix(0) + far[1]) + (far[0] + far[2])
    others = [shifted(mine, "lat", shift) for shift in (1, 2, 3)]
    v_second = lat_back(size, place, s_modes, first_weight, 1)
    others, v_first, v_second = lax.optimization_barrier((others, v_first, v_second))
    own = jnp.stack([mine] + others)
    chips = [crossed(own, "lon", mask) for mask in (2, 4, 6)]
    near = crossed(own, "lon", 1)
    out = lon_back(size, width, [v_first, v_second])
    chips, near, out = lax.optimization_barrier((chips, near, out))
    rest = [crossed(chip, "lon", 1) for chip in chips]
    parts = [own, near, chips[0], rest[0], chips[1], rest[1], chips[2], rest[2]]
    weight_one, weight_two, bias_one, bias_two = assemble(place, parts, width)
    grad_input = out.reshape(lat_rows * lon_cols, width).T.reshape(1, width, lat_rows, lon_cols)
    return (grad_input, weight_one, bias_one, weight_two, bias_two)


def tables(length, count, limit):
    first = jnp.arange(length, dtype=jnp.int32)[:, None]
    second = jnp.arange(count, dtype=jnp.int32)[None, :]
    angle = 2.0 * math.pi / length * (first * second % length).astype(jnp.float32)
    keeper = (second < limit).astype(jnp.float32) / math.sqrt(length)
    return (jnp.cos(angle) * keeper, jnp.sin(angle) * keeper)


def cotangent_weight(length, count):
    index = jnp.arange(count, dtype=jnp.int32)
    edge = (index == 0) | (2 * index == length)
    return jnp.where(edge, 1.0, 2.0).astype(jnp.float32)


def gelu_slope(value):
    inner = GELU_SCALE * (value + GELU_CUBE * value * value * value)
    tangent = jnp.tanh(inner)
    return 0.5 * (1.0 + tangent) + 0.5 * value * (1.0 - tangent * tangent) * GELU_SCALE * (
        1.0 + 3.0 * GELU_CUBE * value * value
    )


def complex_matrix(weight):
    real_part = weight[0]
    imag_part = weight[1]
    upper = jnp.stack([real_part, imag_part], axis=1)
    lower = jnp.stack([-imag_part, real_part], axis=1)
    return jnp.stack([upper, lower], axis=0)


def forward_mix(left, matrix):
    return jnp.einsum("psir,piqj->qsjr", left, matrix, precision=PRECISION)


def back_mix(left, matrix):
    return jnp.einsum("qsjr,piqj->psir", left, matrix, precision=PRECISION)


def weight_grad(left, right):
    total = jnp.einsum("psir,qsjr->piqj", left, right, precision=PRECISION)
    return jnp.stack(
        [total[0, :, 0, :] + total[1, :, 1, :], total[0, :, 1, :] - total[1, :, 0, :]]
    )


def bias_view(vector):
    return vector[:, None, :, None]


def block_backward(x_both, g_both, first_weight, first_bias, second_weight, second_bias):
    first_matrix = complex_matrix(first_weight)
    second_matrix = complex_matrix(second_weight)
    a_both = forward_mix(x_both, first_matrix) + bias_view(first_bias)
    o_both = jax.nn.gelu(a_both, approximate=True)
    z_both = forward_mix(o_both, second_matrix) + bias_view(second_bias)
    e_both = g_both * jnp.tanh(z_both / SHRINK) ** 2
    grad_w_two = weight_grad(o_both, e_both)
    grad_b_two = jnp.sum(e_both, axis=(1, 3))
    s_both = back_mix(e_both, second_matrix) * gelu_slope(a_both)
    grad_w_one = weight_grad(x_both, s_both)
    grad_b_one = jnp.sum(s_both, axis=(1, 3))
    d_both = back_mix(s_both, first_matrix)
    return d_both, (grad_w_one, grad_b_one, grad_w_two, grad_b_two)


def spread_block(layer_input, grad_output, first_weight, first_bias, second_weight, second_bias):
    lon_count = lax.axis_size("lon")
    samples, local_ch, lat_rows, lon_cols = layer_input.shape
    blocks, width = first_weight.shape[1], first_weight.shape[2]
    group = width // local_ch
    groups = [list(range(at, at + group)) for at in range(0, lon_count, group)]
    block = lax.axis_index("lon") // group
    kept_freqs = lon_cols // 2 + 1
    freq_slots = -(-kept_freqs // group) * group
    lon_cos, lon_sin = tables(lon_cols, freq_slots, kept_freqs)
    factor_row = cotangent_weight(lon_cols, freq_slots)[None, :]
    lon_table = jnp.stack([lon_cos, -lon_sin], axis=1)
    cot_table = jnp.stack([lon_cos * factor_row, -lon_sin * factor_row], axis=1)
    lon_back = jnp.stack([lon_cos.T, -lon_sin.T])
    lat_cos, lat_sin = tables(lat_rows, lat_rows, lat_rows)
    lat_table = jnp.stack(
        [jnp.stack([lat_cos, -lat_sin], axis=1), jnp.stack([lat_sin, lat_cos], axis=1)]
    )
    lat_back = jnp.stack(
        [jnp.stack([lat_cos, lat_sin], axis=1), jnp.stack([-lat_sin, lat_cos], axis=1)]
    )

    def spectrum(data, table):
        half = jnp.einsum("schw,wqk->qsckh", data, table, precision=PRECISION)
        full = jnp.einsum("psckh,phqm->qsckm", half, lat_table, precision=PRECISION)
        return full.reshape((2, samples, local_ch, freq_slots * lat_rows))

    def share(data, split, concat):
        if group == 1:
            return data
        return lax.all_to_all(
            data, "lon", split_axis=split, concat_axis=concat, axis_index_groups=groups, tiled=True
        )

    x_modes = share(spectrum(layer_input, lon_table), 3, 2)
    g_modes = share(spectrum(grad_output, cot_table), 3, 2)

    def mine(weight):
        return lax.dynamic_index_in_dim(weight, block, axis=1, keepdims=False)

    d_modes, partial_grads = block_backward(
        x_modes, g_modes, mine(first_weight), mine(first_bias), mine(second_weight), mine(second_bias)
    )
    flat_grads = jnp.concatenate([piece.reshape(-1) for piece in partial_grads])
    summed = lax.psum(flat_grads, "lat")
    if group > 1:
        summed = lax.psum(summed, "lon", axis_index_groups=groups)
    whole = lax.all_gather(summed, "lon", axis=0, tiled=False)[::group]
    stacked = share(d_modes, 2, 3)
    shape_five = (2, samples, local_ch, freq_slots, lat_rows)
    grad_input = jnp.einsum(
        "qsckh,qkw->schw",
        jnp.einsum("psckm,pmqh->qsckh", stacked.reshape(shape_five), lat_back, precision=PRECISION),
        lon_back,
        precision=PRECISION,
    )
    results = []
    offset = 0
    for piece in partial_grads:
        part = whole[:, offset : offset + piece.size].reshape((blocks,) + piece.shape)
        results.append(jnp.moveaxis(part, 0, 1))
        offset = offset + piece.size
    grad_w_one, grad_b_one, grad_w_two, grad_b_two = results
    return (grad_input, grad_w_one, grad_b_one, grad_w_two, grad_b_two)


def on_device(layer_input, grad_output, first_weight, first_bias, second_weight, second_bias):
    samples, local_ch, lat_rows, lon_cols = layer_input.shape
    width = first_weight.shape[2]
    one_device = samples == 1 and local_ch == width <= LANES and width % SUB == 0
    one_device = one_device and lax.axis_size("lat") == 4 and lax.axis_size("lon") == 8
    run = whole_block if one_device and Sizes(lat_rows, lon_cols).fits() else spread_block
    return run(layer_input, grad_output, first_weight, first_bias, second_weight, second_bias)


def solution(mesh):
    placed = (P("lat", "lon", None, None), P("lat", "lon", None, None), P(), P(), P(), P())
    return jax.shard_map(
        on_device,
        mesh=mesh,
        in_specs=placed,
        out_specs=(P("lat", "lon", None, None), P(), P(), P(), P()),
        check_vma=False,
    )
```

```python
import functools
import math

import jax
import jax.numpy as jnp
import ml_dtypes
import numpy as np
from jax import lax
from jax.experimental import pallas as pl
from jax.experimental.pallas import tpu as pltpu
from jax.sharding import PartitionSpec as P

SHRINK = 0.01
GELU_SCALE = math.sqrt(2.0 / math.pi)
GELU_CUBE = 0.044715
PRECISION = lax.Precision.HIGH
LANES = 128
SUB = 8
F32 = jnp.float32
BF16 = jnp.bfloat16
CHUNK = 4
LATS = 16
BAND_MOST = 18
PARTS = 2
GRADIENT_VMEM = 54 << 20
LAT_VMEM = 46 << 20
LON_VMEM = 24 << 20


def round_up(value, unit):
    return -(-value // unit) * unit


def halves(table):
    high = table.astype(ml_dtypes.bfloat16)
    low = (table - high.astype(np.float64)).astype(ml_dtypes.bfloat16)
    return high, low


def split(value):
    high = value.astype(BF16)
    return high, (value - high.astype(F32)).astype(BF16)


def dot(left, right):
    return jnp.dot(left, right, preferred_element_type=F32)


def side_by_side(left, right):
    return jnp.concatenate([left, right], axis=1)


def trig(length, count):
    first = np.arange(count)[:, None]
    second = np.arange(length)[None, :]
    angle = 2.0 * np.pi / length * (first * second % length)
    return np.cos(angle) / math.sqrt(length), np.sin(angle) / math.sqrt(length)


class Sizes:
    def __init__(self, rows, cols):
        self.rows, self.cols = rows, cols
        self.pairs = rows // 2 + 1
        self.half = round_up(self.pairs, SUB)
        self.both = 2 * self.half
        self.freqs = cols // 2 + 1
        self.slots = round_up(self.freqs, 16)
        self.stride = round_up(2 * self.slots, 2 * SUB) + SUB
        self.row_slots = round_up(rows, 16)
        self.col_slots = round_up(cols, 16)
        self.band = max((n for n in range(2, BAND_MOST + 1, 2) if rows % n == 0 and n * cols % SUB == 0), default=0)
        self.batch = SUB

    def fits(self):
        return self.band > 0 and self.cols % 4 == 0


def lat_table(size, cotangent):
    cos, sin = trig(size.rows, size.pairs)
    if cotangent:
        own = np.array([2 * m % size.rows == 0 for m in range(size.pairs)])
        cos, sin = (part * np.where(own, 0.5, 1.0)[:, None] for part in (cos, sin))
    table = np.zeros((size.both, size.row_slots))
    table[: size.pairs, : size.rows] = cos
    table[size.half : size.half + size.pairs, : size.rows] = sin
    return table


def lon_table(size, cotangent):
    cos, sin = trig(size.cols, size.freqs)
    if cotangent:
        index = np.arange(size.freqs)
        factor = np.where((index == 0) | (2 * index == size.cols), 1.0, 2.0)[:, None]
        cos, sin = cos * factor, sin * factor
    table = np.zeros((2 * size.slots, size.col_slots))
    table[: size.freqs, : size.cols] = cos
    table[size.slots : size.slots + size.freqs, : size.cols] = sin
    return table


def four_way(table):
    high, low = halves(table)
    return np.concatenate([np.concatenate([high, high], 1), np.concatenate([low, low], 1)], 0)


def three_way(table):
    high, low = halves(table)
    return np.concatenate([high, low, high], 1)


def four_product(table_ref, data):
    two = dot(table_ref[...], jnp.concatenate(split(data), axis=0))
    count = two.shape[0] // 2
    return two[:count] + two[count:]


def three_product(table_ref, high, low):
    return dot(table_ref[...], jnp.concatenate([high, high, low], axis=0))


def mix(weight_ref, which, high, low):
    return dot(jnp.concatenate([high, low, high], axis=1), weight_ref[which])


def fill_matrix(out, width, real, imag, turned, scale=1.0):
    if turned:
        real, imag = real.T, imag.T
    real, imag = real * scale, imag * scale
    sign = -1.0 if turned else 1.0
    span = 2 * LANES
    for row, column, value in ((0, 0, real), (1, 1, real), (0, 1, sign * imag), (1, 0, -sign * imag)):
        high, low = split(value)
        columns = slice(column * LANES, column * LANES + width)
        for third, part in enumerate((high, high, low)):
            at = third * span + row * LANES
            out[at : at + width, columns] = part


def gradient_kernel(
    size, width, bands, batches, at_ref, x_ref, g_ref, tx_ref, tg_ref, fx_ref, fg_ref, wa_ref, wb_ref, ba_ref, bb_ref,
    s_ref, grad_ref, fold, spectra, keep, plain, total, bias_total, w_ref, b_ref,
):
    step = pl.program_id(0)
    cols, slots, both, half = size.cols, size.slots, size.both, size.half
    stride = size.stride
    lines = 2 * slots
    rows = size.batch * both

    @pl.when(step == 0)
    def _():
        fold[...] = jnp.zeros_like(fold)
        total[...] = jnp.zeros_like(total)
        bias_total[...] = jnp.zeros_like(bias_total)
        w_ref[...] = jnp.zeros_like(w_ref)
        b_ref[...] = jnp.zeros_like(b_ref)
        fill_matrix(w_ref.at[0], width, wa_ref[0, 0], wa_ref[1, 0], False)
        fill_matrix(w_ref.at[1], width, wb_ref[0, 0], wb_ref[1, 0], False, 1.0 / SHRINK)
        fill_matrix(w_ref.at[2], width, wb_ref[0, 0], wb_ref[1, 0], True)
        for layer, (bias, scale) in enumerate(((ba_ref, 1.0), (bb_ref, 1.0 / SHRINK))):
            for q in range(2):
                row = bias[q, pl.ds(at_ref[1], 1), :] * scale
                b_ref[layer, :, q * LANES : q * LANES + width] = jnp.broadcast_to(row, (SUB, width))
        for which in range(2):
            spectra[which, size.rows * stride :] = jnp.zeros(((size.row_slots - size.rows) * stride, LANES), F32)

    @pl.when(step < bands)
    def _():
        for which, (field, table) in enumerate(((x_ref, tx_ref), (g_ref, tg_ref))):
            data = field.reshape(size.band * cols, width)
            for pair in range(size.band // 2):
                slot = which * (size.band // 2) + pair
                for i in range(2):
                    at = (2 * pair + i) * cols
                    high, low = split(data[at : at + cols, :])
                    fold[slot, 0, :cols, i * LANES : i * LANES + width] = high
                    fold[slot, 1, :cols, i * LANES : i * LANES + width] = low
                out = three_product(table, fold[slot, 0], fold[slot, 1])
                for i in range(2):
                    base = pl.multiple_of((step * size.band + 2 * pair + i) * stride, SUB)
                    spectra[which, pl.ds(base, lines), :] = out[:, i * LANES : (i + 1) * LANES]

    @pl.when(step >= bands)
    def _():
        first = (step - bands) * size.batch
        span = CHUNK * both
        piece = 16

        def transform(chunk):
            for k in range(chunk * CHUNK, (chunk + 1) * CHUNK):
                at = k * both
                for which, table in enumerate((fx_ref, fg_ref)):
                    data = side_by_side(
                        spectra[which, pl.ds(first + k, size.row_slots, stride=stride), :],
                        spectra[which, pl.ds(first + k + slots, size.row_slots, stride=stride), :],
                    )
                    out = four_product(table, data)
                    cos_one, cos_two = out[:half, :LANES], out[:half, LANES:]
                    sin_one, sin_two = out[half:, :LANES], out[half:, LANES:]
                    plus = side_by_side(cos_one - sin_two, -(cos_two + sin_one))
                    minus = side_by_side(cos_one + sin_two, sin_one - cos_two)
                    for part, value in ((0, plus), (1, minus)):
                        here = slice(at + part * half, at + (part + 1) * half)
                        if which == 0:
                            keep_split(0, here, value)
                        else:
                            plain[0, here] = value

        def keep_split(which, here, value):
            high, low = split(value)
            keep[which, 0, here] = high
            keep[which, 1, here] = low

        def multiply(which, chunk):
            here = slice(chunk * span, (chunk + 1) * span)
            plain[1 + which, here] = mix(w_ref, which, keep[which, 0, here], keep[which, 1, here])

        def pieces(chunk):
            return [slice(at, at + piece) for at in range(chunk * span, (chunk + 1) * span, piece)]

        def activate(chunk):
            for here in pieces(chunk):
                a = plain[1, here] + b_ref[0, :1]
                square = a * a
                tangent = jnp.tanh(a * (GELU_SCALE + (GELU_SCALE * GELU_CUBE) * square))
                share = 0.5 * tangent + 0.5
                o = a * share
                plain[1, here] = share + (o - o * share) * (
                    2.0 * GELU_SCALE + (6.0 * GELU_SCALE * GELU_CUBE) * square
                )
                keep_split(1, here, o)

        def gate(chunk):
            sums = jnp.zeros((SUB, 2 * LANES), F32)
            for here in pieces(chunk):
                tangent = jnp.tanh(plain[2, here] + b_ref[1, :1])
                e = plain[0, here] * (tangent * tangent)
                for i in range(0, piece, SUB):
                    sums = sums + e[i : i + SUB]
                keep_split(2, here, e)
            bias_total[1] += sums

        def slope(chunk):
            sums = jnp.zeros((SUB, 2 * LANES), F32)
            for here in pieces(chunk):
                value = plain[3, here] * plain[1, here]
                s_ref[here] = value
                for i in range(0, piece, SUB):
                    sums = sums + value[i : i + SUB]
                keep_split(3, here, value)
            bias_total[0] += sums

        def turned(which):
            parts = [keep[which, i].T for i in range(2)]
            return [jnp.concatenate([part[:width], part[LANES : LANES + width]], axis=0) for part in parts]

        def weight_grad(layer, left, right):
            high, low = turned(left)
            total[layer] += dot(
                jnp.concatenate([high, low, high], axis=1),
                jnp.concatenate([keep[right, 0], keep[right, 0], keep[right, 1]], axis=0),
            )

        count = size.batch // CHUNK
        for t in range(count + 3):
            if t < count:
                transform(t)
                multiply(0, t)
            if 0 <= t - 1 < count:
                activate(t - 1)
                multiply(1, t - 1)
            if 0 <= t - 2 < count:
                gate(t - 2)
                multiply(2, t - 2)
            if 0 <= t - 3 < count:
                slope(t - 3)
        weight_grad(1, 1, 2)
        weight_grad(0, 0, 3)

    @pl.when(step == bands + batches - 1)
    def _():
        for layer in range(2):
            upper = total[layer, :width]
            lower = total[layer, width:]
            grad_ref[layer, 0, :width] = upper[:, :LANES] + lower[:, LANES:]
            grad_ref[layer, 1, :width] = upper[:, LANES:] - lower[:, :LANES]
            bias = jnp.broadcast_to(jnp.sum(bias_total[layer], axis=0, keepdims=True), (SUB, 2 * LANES))
            grad_ref[layer, 0, width:] = bias[:, :LANES]
            grad_ref[layer, 1, width:] = bias[:, LANES:]


def lat_back_kernel(size, width, at_ref, s_ref, wa_ref, f_ref, v_ref, plain, w_ref):
    both, half = size.both, size.half
    span = CHUNK * both

    @pl.when(pl.program_id(0) == 0)
    def _():
        w_ref[...] = jnp.zeros_like(w_ref)
        fill_matrix(w_ref.at[0], width, wa_ref[0, 0], wa_ref[1, 0], True)

    def multiply(chunk):
        here = slice(chunk * span, (chunk + 1) * span)
        plain[here] = mix(w_ref, 0, *split(s_ref[here]))

    def transform(chunk):
        for k in range(chunk * CHUNK, (chunk + 1) * CHUNK):
            at = k * both
            plus, minus = plain[at : at + half], plain[at + half : at + both]
            add, sub = plus + minus, plus - minus
            data = jnp.concatenate(
                [
                    side_by_side(add[:, :LANES], -add[:, LANES:]),
                    side_by_side(sub[:, LANES:], sub[:, :LANES]),
                ],
                axis=0,
            )
            out = four_product(f_ref, data)
            for q in range(2):
                v_ref[q, k] = out[:, q * LANES : (q + 1) * LANES]

    count = size.batch // CHUNK
    for t in range(count + 1):
        if t < count:
            multiply(t)
        if t > 0:
            transform(t - 1)


def lon_back_kernel(size, width, *refs):
    v_refs, (t_ref, out_ref) = refs[:PARTS], refs[PARTS:]
    cols = size.cols
    lines = size.slots // PARTS
    flat = out_ref.reshape(LATS * cols, width)
    rows = [ref.reshape(2 * lines * LATS, LANES) for ref in v_refs]
    for pair in range(LATS // 2):
        data = side_by_side(
            *(
                jnp.concatenate(
                    [
                        part[pl.ds(q * lines * LATS + 2 * pair + i, lines, stride=LATS), :]
                        for q in range(2)
                        for part in rows
                    ],
                    axis=0,
                )
                for i in range(2)
            )
        )
        out = three_product(t_ref, *split(data))
        for i in range(2):
            at = (2 * pair + i) * cols
            flat[at : at + cols, :] = out[:cols, i * LANES : i * LANES + width]


def assemble_kernel(width, count, at_ref, *refs):
    parts, (wa_ref, wb_ref, ba_ref, bb_ref) = refs[:count], refs[count:]
    for l, (weight, bias) in enumerate(((wa_ref, ba_ref), (wa_ref, ba_ref), (wb_ref, bb_ref), (wb_ref, bb_ref))):
        shift = lax.rem(at_ref[0] + 4 - l, 4)
        for x in range(count):
            block = at_ref[2 + x]
            weight[l % 2, block] = parts[x][shift, :width, :width]
            bias[l % 2, pl.ds(block, 1), :] = parts[x][shift, width : width + 1, :width]


def whole_spec(array):
    zeros = (0,) * array.ndim
    return pl.BlockSpec(array.shape, lambda *_: zeros)


def spectral_gradients(size, place, fields, first_weight, first_bias, second_weight, second_bias):
    width = first_weight.shape[-1]
    tables = [three_way(lon_table(size, which)) for which in (False, True)]
    tables += [four_way(lat_table(size, which)) for which in (False, True)]
    consts = [jnp.asarray(table) for table in tables]
    weight = pl.BlockSpec((2, 1, width, width), lambda i, at: (0, at[1], 0, 0))
    bias = whole_spec(first_bias)
    bands, batches = size.rows // size.band, size.slots // size.batch
    rows = size.batch * size.both
    field = pl.BlockSpec((size.band * size.cols // SUB, SUB, width), lambda i, at: (jnp.minimum(i, bands - 1), 0, 0))
    return pl.pallas_call(
        functools.partial(gradient_kernel, size, width, bands, batches),
        grid_spec=pltpu.PrefetchScalarGridSpec(
            num_scalar_prefetch=1,
            grid=(bands + batches,),
            in_specs=[field, field] + [whole_spec(const) for const in consts] + [weight, weight, bias, bias],
            out_specs=[
                pl.BlockSpec((rows, 2 * LANES), lambda i, at: (jnp.maximum(i - bands, 0), 0)),
                pl.BlockSpec((2, 2, width + SUB, LANES), lambda i, at: (0, 0, 0, 0)),
            ],
            scratch_shapes=[
                pltpu.VMEM((size.band, 2, size.col_slots, 2 * LANES), BF16),
                pltpu.VMEM((2, size.row_slots * size.stride, LANES), F32),
                pltpu.VMEM((4, 2, rows, 2 * LANES), BF16),
                pltpu.VMEM((4, rows, 2 * LANES), F32),
                pltpu.VMEM((2, 2 * width, 2 * LANES), F32),
                pltpu.VMEM((2, SUB, 2 * LANES), F32),
                pltpu.VMEM((3, 6 * LANES, 2 * LANES), BF16),
                pltpu.VMEM((2, SUB, 2 * LANES), F32),
            ],
        ),
        out_shape=[
            jax.ShapeDtypeStruct((size.slots * size.both, 2 * LANES), F32),
            jax.ShapeDtypeStruct((2, 2, width + SUB, LANES), F32),
        ],
        compiler_params=pltpu.CompilerParams(vmem_limit_bytes=GRADIENT_VMEM),
        name="spectral_gradients",
    )(place, *fields, *consts, first_weight, second_weight, first_bias, second_bias)


def lat_back(size, place, s_modes, weight, part):
    width = weight.shape[-1]
    lat = lat_table(size, False).T.copy()
    lat[:, size.half :] *= -1.0
    table = jnp.asarray(four_way(lat))
    rows = size.batch * size.both
    steps = size.slots // size.batch // PARTS
    return pl.pallas_call(
        functools.partial(lat_back_kernel, size, width),
        grid_spec=pltpu.PrefetchScalarGridSpec(
            num_scalar_prefetch=1,
            grid=(steps,),
            in_specs=[
                pl.BlockSpec((rows, 2 * LANES), lambda i, at: (part * steps + i, 0)),
                pl.BlockSpec((2, 1, width, width), lambda i, at: (0, at[1], 0, 0)),
                whole_spec(table),
            ],
            out_specs=pl.BlockSpec((2, size.batch, size.row_slots, LANES), lambda i, at: (0, i, 0, 0)),
            scratch_shapes=[pltpu.VMEM((rows, 2 * LANES), F32), pltpu.VMEM((1, 6 * LANES, 2 * LANES), BF16)],
        ),
        out_shape=jax.ShapeDtypeStruct((2, size.slots // PARTS, size.row_slots, LANES), F32),
        compiler_params=pltpu.CompilerParams(vmem_limit_bytes=LAT_VMEM),
        name="lat_back",
    )(place, s_modes, weight, table)


def lon_back(size, width, v_parts):
    table = jnp.asarray(three_way(lon_table(size, False).T))
    field = pl.BlockSpec((2, size.slots // PARTS, LATS, LANES), lambda i: (0, 0, i, 0))
    return pl.pallas_call(
        functools.partial(lon_back_kernel, size, width),
        grid=(size.row_slots // LATS,),
        in_specs=[field] * PARTS + [whole_spec(table)],
        out_specs=pl.BlockSpec((size.cols * LATS // SUB, SUB, width), lambda i: (i, 0, 0)),
        out_shape=jax.ShapeDtypeStruct((size.rows * size.cols // SUB, SUB, width), F32),
        compiler_params=pltpu.CompilerParams(vmem_limit_bytes=LON_VMEM),
        name="lon_back",
    )(*v_parts, table)


def assemble(place, parts, width):
    count = len(parts)
    shapes = [(2, count, width, width)] * 2 + [(2, count, width)] * 2
    memory = pl.BlockSpec(memory_space=pltpu.VMEM)
    return pl.pallas_call(
        functools.partial(assemble_kernel, width, count),
        in_specs=[pl.BlockSpec(memory_space=pltpu.SMEM)] + [memory] * count,
        out_specs=[memory] * 4,
        out_shape=[jax.ShapeDtypeStruct(shape, F32) for shape in shapes],
        compiler_params=pltpu.CompilerParams(vmem_limit_bytes=LON_VMEM),
        name="assemble",
    )(place, *parts)


def shifted(value, axis, shift):
    count = lax.axis_size(axis)
    return lax.ppermute(value, axis, [(i, (i + shift) % count) for i in range(count)])


def crossed(value, axis, mask):
    count = lax.axis_size(axis)
    return lax.ppermute(value, axis, [(i, i ^ mask) for i in range(count)])


def whole_block(layer_input, grad_output, first_weight, first_bias, second_weight, second_bias):
    _, width, lat_rows, lon_cols = layer_input.shape
    size = Sizes(lat_rows, lon_cols)
    at_lat, at_lon = lax.axis_index("lat"), lax.axis_index("lon")
    place = jnp.stack([at_lat, at_lon] + [at_lon ^ x for x in range(lax.axis_size("lon"))])
    fields = [
        jnp.transpose(field, (0, 2, 3, 1)).reshape(-1, SUB, width) for field in (layer_input, grad_output)
    ]
    s_modes, partial = spectral_gradients(
        size, place, fields, first_weight, first_bias, second_weight, second_bias
    )
    matrices = partial.reshape(4, width + SUB, LANES)

    def matrix(shift):
        return lax.dynamic_index_in_dim(matrices, (at_lat + shift) % 4, 0, keepdims=False)

    far = [shifted(matrix(shift), "lat", shift) for shift in (1, 2, 3)]
    v_first = lat_back(size, place, s_modes, first_weight, 0)
    far, v_first, s_modes = lax.optimization_barrier((far, v_first, s_modes))
    mine = (matrix(0) + far[1]) + (far[0] + far[2])
    others = [shifted(mine, "lat", shift) for shift in (1, 2, 3)]
    v_second = lat_back(size, place, s_modes, first_weight, 1)
    others, v_first, v_second = lax.optimization_barrier((others, v_first, v_second))
    own = jnp.stack([mine] + others)
    chips = [crossed(own, "lon", mask) for mask in (2, 4, 6)]
    near = crossed(own, "lon", 1)
    out = lon_back(size, width, [v_first, v_second])
    chips, near, out = lax.optimization_barrier((chips, near, out))
    rest = [crossed(chip, "lon", 1) for chip in chips]
    parts = [own, near, chips[0], rest[0], chips[1], rest[1], chips[2], rest[2]]
    weight_one, weight_two, bias_one, bias_two = assemble(place, parts, width)
    grad_input = out.reshape(lat_rows * lon_cols, width).T.reshape(1, width, lat_rows, lon_cols)
    return (grad_input, weight_one, bias_one, weight_two, bias_two)


def tables(length, count, limit):
    first = jnp.arange(length, dtype=jnp.int32)[:, None]
    second = jnp.arange(count, dtype=jnp.int32)[None, :]
    angle = 2.0 * math.pi / length * (first * second % length).astype(jnp.float32)
    keeper = (second < limit).astype(jnp.float32) / math.sqrt(length)
    return (jnp.cos(angle) * keeper, jnp.sin(angle) * keeper)


def cotangent_weight(length, count):
    index = jnp.arange(count, dtype=jnp.int32)
    edge = (index == 0) | (2 * index == length)
    return jnp.where(edge, 1.0, 2.0).astype(jnp.float32)


def gelu_slope(value):
    inner = GELU_SCALE * (value + GELU_CUBE * value * value * value)
    tangent = jnp.tanh(inner)
    return 0.5 * (1.0 + tangent) + 0.5 * value * (1.0 - tangent * tangent) * GELU_SCALE * (
        1.0 + 3.0 * GELU_CUBE * value * value
    )


def complex_matrix(weight):
    real_part = weight[0]
    imag_part = weight[1]
    upper = jnp.stack([real_part, imag_part], axis=1)
    lower = jnp.stack([-imag_part, real_part], axis=1)
    return jnp.stack([upper, lower], axis=0)


def forward_mix(left, matrix):
    return jnp.einsum("psir,piqj->qsjr", left, matrix, precision=PRECISION)


def back_mix(left, matrix):
    return jnp.einsum("qsjr,piqj->psir", left, matrix, precision=PRECISION)


def weight_grad(left, right):
    total = jnp.einsum("psir,qsjr->piqj", left, right, precision=PRECISION)
    return jnp.stack(
        [total[0, :, 0, :] + total[1, :, 1, :], total[0, :, 1, :] - total[1, :, 0, :]]
    )


def bias_view(vector):
    return vector[:, None, :, None]


def block_backward(x_both, g_both, first_weight, first_bias, second_weight, second_bias):
    first_matrix = complex_matrix(first_weight)
    second_matrix = complex_matrix(second_weight)
    a_both = forward_mix(x_both, first_matrix) + bias_view(first_bias)
    o_both = jax.nn.gelu(a_both, approximate=True)
    z_both = forward_mix(o_both, second_matrix) + bias_view(second_bias)
    e_both = g_both * jnp.tanh(z_both / SHRINK) ** 2
    grad_w_two = weight_grad(o_both, e_both)
    grad_b_two = jnp.sum(e_both, axis=(1, 3))
    s_both = back_mix(e_both, second_matrix) * gelu_slope(a_both)
    grad_w_one = weight_grad(x_both, s_both)
    grad_b_one = jnp.sum(s_both, axis=(1, 3))
    d_both = back_mix(s_both, first_matrix)
    return d_both, (grad_w_one, grad_b_one, grad_w_two, grad_b_two)


def spread_block(layer_input, grad_output, first_weight, first_bias, second_weight, second_bias):
    lon_count = lax.axis_size("lon")
    samples, local_ch, lat_rows, lon_cols = layer_input.shape
    blocks, width = first_weight.shape[1], first_weight.shape[2]
    group = width // local_ch
    groups = [list(range(at, at + group)) for at in range(0, lon_count, group)]
    block = lax.axis_index("lon") // group
    kept_freqs = lon_cols // 2 + 1
    freq_slots = -(-kept_freqs // group) * group
    lon_cos, lon_sin = tables(lon_cols, freq_slots, kept_freqs)
    factor_row = cotangent_weight(lon_cols, freq_slots)[None, :]
    lon_table = jnp.stack([lon_cos, -lon_sin], axis=1)
    cot_table = jnp.stack([lon_cos * factor_row, -lon_sin * factor_row], axis=1)
    lon_back = jnp.stack([lon_cos.T, -lon_sin.T])
    lat_cos, lat_sin = tables(lat_rows, lat_rows, lat_rows)
    lat_table = jnp.stack(
        [jnp.stack([lat_cos, -lat_sin], axis=1), jnp.stack([lat_sin, lat_cos], axis=1)]
    )
    lat_back = jnp.stack(
        [jnp.stack([lat_cos, lat_sin], axis=1), jnp.stack([-lat_sin, lat_cos], axis=1)]
    )

    def spectrum(data, table):
        half = jnp.einsum("schw,wqk->qsckh", data, table, precision=PRECISION)
        full = jnp.einsum("psckh,phqm->qsckm", half, lat_table, precision=PRECISION)
        return full.reshape((2, samples, local_ch, freq_slots * lat_rows))

    def share(data, split, concat):
        if group == 1:
            return data
        return lax.all_to_all(
            data, "lon", split_axis=split, concat_axis=concat, axis_index_groups=groups, tiled=True
        )

    x_modes = share(spectrum(layer_input, lon_table), 3, 2)
    g_modes = share(spectrum(grad_output, cot_table), 3, 2)

    def mine(weight):
        return lax.dynamic_index_in_dim(weight, block, axis=1, keepdims=False)

    d_modes, partial_grads = block_backward(
        x_modes, g_modes, mine(first_weight), mine(first_bias), mine(second_weight), mine(second_bias)
    )
    flat_grads = jnp.concatenate([piece.reshape(-1) for piece in partial_grads])
    summed = lax.psum(flat_grads, "lat")
    if group > 1:
        summed = lax.psum(summed, "lon", axis_index_groups=groups)
    whole = lax.all_gather(summed, "lon", axis=0, tiled=False)[::group]
    stacked = share(d_modes, 2, 3)
    shape_five = (2, samples, local_ch, freq_slots, lat_rows)
    grad_input = jnp.einsum(
        "qsckh,qkw->schw",
        jnp.einsum("psckm,pmqh->qsckh", stacked.reshape(shape_five), lat_back, precision=PRECISION),
        lon_back,
        precision=PRECISION,
    )
    results = []
    offset = 0
    for piece in partial_grads:
        part = whole[:, offset : offset + piece.size].reshape((blocks,) + piece.shape)
        results.append(jnp.moveaxis(part, 0, 1))
        offset = offset + piece.size
    grad_w_one, grad_b_one, grad_w_two, grad_b_two = results
    return (grad_input, grad_w_one, grad_b_one, grad_w_two, grad_b_two)


def on_device(layer_input, grad_output, first_weight, first_bias, second_weight, second_bias):
    samples, local_ch, lat_rows, lon_cols = layer_input.shape
    width = first_weight.shape[2]
    one_device = samples == 1 and local_ch == width <= LANES and width % SUB == 0
    one_device = one_device and lax.axis_size("lat") == 4 and lax.axis_size("lon") == 8
    run = whole_block if one_device and Sizes(lat_rows, lon_cols).fits() else spread_block
    return run(layer_input, grad_output, first_weight, first_bias, second_weight, second_bias)


def solution(mesh):
    placed = (P("lat", "lon", None, None), P("lat", "lon", None, None), P(), P(), P(), P())
    return jax.shard_map(
        on_device,
        mesh=mesh,
        in_specs=placed,
        out_specs=(P("lat", "lon", None, None), P(), P(), P(), P()),
        check_vma=False,
    )
```

```python
import functools
import math

import jax
import jax.numpy as jnp
import ml_dtypes
import numpy as np
from jax import lax
from jax.experimental import pallas as pl
from jax.experimental.pallas import tpu as pltpu
from jax.sharding import PartitionSpec as P

SHRINK = 0.01
GELU_SCALE = math.sqrt(2.0 / math.pi)
GELU_CUBE = 0.044715
PRECISION = lax.Precision.HIGH
LANES = 128
SUB = 8
F32 = jnp.float32
BF16 = jnp.bfloat16
CHUNK = 4
LATS = 16
BAND_MOST = 18
PARTS = 2
GRADIENT_VMEM = 54 << 20
LAT_VMEM = 46 << 20
LON_VMEM = 24 << 20


def round_up(value, unit):
    return -(-value // unit) * unit


def halves(table):
    high = table.astype(ml_dtypes.bfloat16)
    low = (table - high.astype(np.float64)).astype(ml_dtypes.bfloat16)
    return high, low


def split(value):
    high = value.astype(BF16)
    return high, (value - high.astype(F32)).astype(BF16)


def dot(left, right):
    return jnp.dot(left, right, preferred_element_type=F32)


def side_by_side(left, right):
    return jnp.concatenate([left, right], axis=1)


def trig(length, count):
    first = np.arange(count)[:, None]
    second = np.arange(length)[None, :]
    angle = 2.0 * np.pi / length * (first * second % length)
    return np.cos(angle) / math.sqrt(length), np.sin(angle) / math.sqrt(length)


class Sizes:
    def __init__(self, rows, cols):
        self.rows, self.cols = rows, cols
        self.pairs = rows // 2 + 1
        self.half = round_up(self.pairs, SUB)
        self.both = 2 * self.half
        self.freqs = cols // 2 + 1
        self.slots = round_up(self.freqs, 16)
        self.stride = round_up(2 * self.slots, 2 * SUB) + SUB
        self.row_slots = round_up(rows, 16)
        self.col_slots = round_up(cols, 16)
        self.band = max((n for n in range(2, BAND_MOST + 1, 2) if rows % n == 0 and n * cols % SUB == 0), default=0)
        self.batch = SUB

    def fits(self):
        return self.band > 0 and self.cols % 4 == 0


def lat_table(size, cotangent):
    cos, sin = trig(size.rows, size.pairs)
    if cotangent:
        own = np.array([2 * m % size.rows == 0 for m in range(size.pairs)])
        cos, sin = (part * np.where(own, 0.5, 1.0)[:, None] for part in (cos, sin))
    table = np.zeros((size.both, size.row_slots))
    table[: size.pairs, : size.rows] = cos
    table[size.half : size.half + size.pairs, : size.rows] = sin
    return table


def lon_table(size, cotangent):
    cos, sin = trig(size.cols, size.freqs)
    if cotangent:
        index = np.arange(size.freqs)
        factor = np.where((index == 0) | (2 * index == size.cols), 1.0, 2.0)[:, None]
        cos, sin = cos * factor, sin * factor
    table = np.zeros((2 * size.slots, size.col_slots))
    table[: size.freqs, : size.cols] = cos
    table[size.slots : size.slots + size.freqs, : size.cols] = sin
    return table


def four_way(table):
    high, low = halves(table)
    return np.concatenate([np.concatenate([high, high], 1), np.concatenate([low, low], 1)], 0)


def three_way(table):
    high, low = halves(table)
    return np.concatenate([high, low, high], 1)


def four_product(table_ref, data):
    two = dot(table_ref[...], jnp.concatenate(split(data), axis=0))
    count = two.shape[0] // 2
    return two[:count] + two[count:]


def three_product(table_ref, high, low):
    return dot(table_ref[...], jnp.concatenate([high, high, low], axis=0))


def mix(weight_ref, which, high, low):
    return dot(jnp.concatenate([high, low, high], axis=1), weight_ref[which])


def fill_matrix(out, width, real, imag, turned, scale=1.0):
    if turned:
        real, imag = real.T, imag.T
    real, imag = real * scale, imag * scale
    sign = -1.0 if turned else 1.0
    span = 2 * LANES
    for row, column, value in ((0, 0, real), (1, 1, real), (0, 1, sign * imag), (1, 0, -sign * imag)):
        high, low = split(value)
        columns = slice(column * LANES, column * LANES + width)
        for third, part in enumerate((high, high, low)):
            at = third * span + row * LANES
            out[at : at + width, columns] = part


def gradient_kernel(
    size, width, bands, batches, at_ref, x_ref, g_ref, tx_ref, tg_ref, fx_ref, fg_ref, wa_ref, wb_ref, ba_ref, bb_ref,
    s_ref, grad_ref, fold, spectra, keep, plain, total, bias_total, w_ref, b_ref,
):
    step = pl.program_id(0)
    cols, slots, both, half = size.cols, size.slots, size.both, size.half
    stride = size.stride
    lines = 2 * slots
    rows = size.batch * both

    @pl.when(step == 0)
    def _():
        fold[...] = jnp.zeros_like(fold)
        total[...] = jnp.zeros_like(total)
        bias_total[...] = jnp.zeros_like(bias_total)
        w_ref[...] = jnp.zeros_like(w_ref)
        b_ref[...] = jnp.zeros_like(b_ref)
        fill_matrix(w_ref.at[0], width, wa_ref[0, 0], wa_ref[1, 0], False)
        fill_matrix(w_ref.at[1], width, wb_ref[0, 0], wb_ref[1, 0], False, 1.0 / SHRINK)
        fill_matrix(w_ref.at[2], width, wb_ref[0, 0], wb_ref[1, 0], True)
        for layer, (bias, scale) in enumerate(((ba_ref, 1.0), (bb_ref, 1.0 / SHRINK))):
            for q in range(2):
                row = bias[q, pl.ds(at_ref[1], 1), :] * scale
                b_ref[layer, :, q * LANES : q * LANES + width] = jnp.broadcast_to(row, (SUB, width))
        for which in range(2):
            spectra[which, size.rows * stride :] = jnp.zeros(((size.row_slots - size.rows) * stride, LANES), F32)

    @pl.when(step < bands)
    def _():
        for which, (field, table) in enumerate(((x_ref, tx_ref), (g_ref, tg_ref))):
            data = field.reshape(size.band * cols, width)
            for pair in range(size.band // 2):
                slot = which * (size.band // 2) + pair
                for i in range(2):
                    at = (2 * pair + i) * cols
                    high, low = split(data[at : at + cols, :])
                    fold[slot, 0, :cols, i * LANES : i * LANES + width] = high
                    fold[slot, 1, :cols, i * LANES : i * LANES + width] = low
                out = three_product(table, fold[slot, 0], fold[slot, 1])
                for i in range(2):
                    base = pl.multiple_of((step * size.band + 2 * pair + i) * stride, SUB)
                    spectra[which, pl.ds(base, lines), :] = out[:, i * LANES : (i + 1) * LANES]

    @pl.when(step >= bands)
    def _():
        first = (step - bands) * size.batch
        span = CHUNK * both
        piece = 16

        def transform(chunk):
            for k in range(chunk * CHUNK, (chunk + 1) * CHUNK):
                at = k * both
                for which, table in enumerate((fx_ref, fg_ref)):
                    data = side_by_side(
                        spectra[which, pl.ds(first + k, size.row_slots, stride=stride), :],
                        spectra[which, pl.ds(first + k + slots, size.row_slots, stride=stride), :],
                    )
                    out = four_product(table, data)
                    cos_one, cos_two = out[:half, :LANES], out[:half, LANES:]
                    sin_one, sin_two = out[half:, :LANES], out[half:, LANES:]
                    plus = side_by_side(cos_one - sin_two, -(cos_two + sin_one))
                    minus = side_by_side(cos_one + sin_two, sin_one - cos_two)
                    for part, value in ((0, plus), (1, minus)):
                        here = slice(at + part * half, at + (part + 1) * half)
                        if which == 0:
                            keep_split(0, here, value)
                        else:
                            plain[0, here] = value

        def keep_split(which, here, value):
            high, low = split(value)
            keep[which, 0, here] = high
            keep[which, 1, here] = low

        def multiply(which, chunk):
            here = slice(chunk * span, (chunk + 1) * span)
            plain[1 + which, here] = mix(w_ref, which, keep[which, 0, here], keep[which, 1, here])

        def pieces(chunk):
            return [slice(at, at + piece) for at in range(chunk * span, (chunk + 1) * span, piece)]

        def activate(chunk):
            for here in pieces(chunk):
                a = plain[1, here] + b_ref[0, :1]
                square = a * a
                tangent = jnp.tanh(a * (GELU_SCALE + (GELU_SCALE * GELU_CUBE) * square))
                share = 0.5 * tangent + 0.5
                o = a * share
                plain[1, here] = share + (o - o * share) * (
                    2.0 * GELU_SCALE + (6.0 * GELU_SCALE * GELU_CUBE) * square
                )
                keep_split(1, here, o)

        def gate(chunk):
            sums = jnp.zeros((SUB, 2 * LANES), F32)
            for here in pieces(chunk):
                tangent = jnp.tanh(plain[2, here] + b_ref[1, :1])
                e = plain[0, here] * (tangent * tangent)
                for i in range(0, piece, SUB):
                    sums = sums + e[i : i + SUB]
                keep_split(2, here, e)
            bias_total[1] += sums

        def slope(chunk):
            sums = jnp.zeros((SUB, 2 * LANES), F32)
            for here in pieces(chunk):
                value = plain[3, here] * plain[1, here]
                s_ref[here] = value
                for i in range(0, piece, SUB):
                    sums = sums + value[i : i + SUB]
                keep_split(3, here, value)
            bias_total[0] += sums

        def turned(which):
            parts = [keep[which, i].T for i in range(2)]
            return [jnp.concatenate([part[:width], part[LANES : LANES + width]], axis=0) for part in parts]

        def weight_grad(layer, left, right):
            high, low = turned(left)
            total[layer] += dot(
                jnp.concatenate([high, low, high], axis=1),
                jnp.concatenate([keep[right, 0], keep[right, 0], keep[right, 1]], axis=0),
            )

        count = size.batch // CHUNK
        for t in range(count + 3):
            if t < count:
                transform(t)
                multiply(0, t)
            if 0 <= t - 1 < count:
                activate(t - 1)
                multiply(1, t - 1)
            if 0 <= t - 2 < count:
                gate(t - 2)
                multiply(2, t - 2)
            if 0 <= t - 3 < count:
                slope(t - 3)
        weight_grad(1, 1, 2)
        weight_grad(0, 0, 3)

    @pl.when(step == bands + batches - 1)
    def _():
        for layer in range(2):
            upper = total[layer, :width]
            lower = total[layer, width:]
            grad_ref[layer, 0, :width] = upper[:, :LANES] + lower[:, LANES:]
            grad_ref[layer, 1, :width] = upper[:, LANES:] - lower[:, :LANES]
            bias = jnp.broadcast_to(jnp.sum(bias_total[layer], axis=0, keepdims=True), (SUB, 2 * LANES))
            grad_ref[layer, 0, width:] = bias[:, :LANES]
            grad_ref[layer, 1, width:] = bias[:, LANES:]


def lat_back_kernel(size, width, at_ref, s_ref, wa_ref, f_ref, v_ref, plain, w_ref):
    both, half = size.both, size.half
    span = CHUNK * both

    @pl.when(pl.program_id(0) == 0)
    def _():
        w_ref[...] = jnp.zeros_like(w_ref)
        fill_matrix(w_ref.at[0], width, wa_ref[0, 0], wa_ref[1, 0], True)

    def multiply(chunk):
        here = slice(chunk * span, (chunk + 1) * span)
        plain[here] = mix(w_ref, 0, *split(s_ref[here]))

    def transform(chunk):
        for k in range(chunk * CHUNK, (chunk + 1) * CHUNK):
            at = k * both
            plus, minus = plain[at : at + half], plain[at + half : at + both]
            add, sub = plus + minus, plus - minus
            data = jnp.concatenate(
                [
                    side_by_side(add[:, :LANES], -add[:, LANES:]),
                    side_by_side(sub[:, LANES:], sub[:, :LANES]),
                ],
                axis=0,
            )
            out = four_product(f_ref, data)
            for q in range(2):
                v_ref[q, k] = out[:, q * LANES : (q + 1) * LANES]

    count = size.batch // CHUNK
    for t in range(count + 1):
        if t < count:
            multiply(t)
        if t > 0:
            transform(t - 1)


def lon_back_kernel(size, width, *refs):
    v_refs, (t_ref, out_ref) = refs[:PARTS], refs[PARTS:]
    cols = size.cols
    lines = size.slots // PARTS
    flat = out_ref.reshape(LATS * cols, width)
    rows = [ref.reshape(2 * lines * LATS, LANES) for ref in v_refs]
    for pair in range(LATS // 2):
        data = side_by_side(
            *(
                jnp.concatenate(
                    [
                        part[pl.ds(q * lines * LATS + 2 * pair + i, lines, stride=LATS), :]
                        for q in range(2)
                        for part in rows
                    ],
                    axis=0,
                )
                for i in range(2)
            )
        )
        out = three_product(t_ref, *split(data))
        for i in range(2):
            at = (2 * pair + i) * cols
            flat[at : at + cols, :] = out[:cols, i * LANES : i * LANES + width]


def assemble_kernel(width, count, at_ref, *refs):
    parts, (wa_ref, wb_ref, ba_ref, bb_ref) = refs[:count], refs[count:]
    for l, (weight, bias) in enumerate(((wa_ref, ba_ref), (wa_ref, ba_ref), (wb_ref, bb_ref), (wb_ref, bb_ref))):
        for x in range(count):
            block = at_ref[2 + x]
            weight[l % 2, block] = parts[x][l, :width, :width]
            bias[l % 2, pl.ds(block, 1), :] = parts[x][l, width : width + 1, :width]


def whole_spec(array):
    zeros = (0,) * array.ndim
    return pl.BlockSpec(array.shape, lambda *_: zeros)


def spectral_gradients(size, place, fields, first_weight, first_bias, second_weight, second_bias):
    width = first_weight.shape[-1]
    tables = [three_way(lon_table(size, which)) for which in (False, True)]
    tables += [four_way(lat_table(size, which)) for which in (False, True)]
    consts = [jnp.asarray(table) for table in tables]
    weight = pl.BlockSpec((2, 1, width, width), lambda i, at: (0, at[1], 0, 0))
    bias = whole_spec(first_bias)
    bands, batches = size.rows // size.band, size.slots // size.batch
    rows = size.batch * size.both
    field = pl.BlockSpec((size.band * size.cols // SUB, SUB, width), lambda i, at: (jnp.minimum(i, bands - 1), 0, 0))
    return pl.pallas_call(
        functools.partial(gradient_kernel, size, width, bands, batches),
        grid_spec=pltpu.PrefetchScalarGridSpec(
            num_scalar_prefetch=1,
            grid=(bands + batches,),
            in_specs=[field, field] + [whole_spec(const) for const in consts] + [weight, weight, bias, bias],
            out_specs=[
                pl.BlockSpec((rows, 2 * LANES), lambda i, at: (jnp.maximum(i - bands, 0), 0)),
                pl.BlockSpec((2, 2, width + SUB, LANES), lambda i, at: (0, 0, 0, 0)),
            ],
            scratch_shapes=[
                pltpu.VMEM((size.band, 2, size.col_slots, 2 * LANES), BF16),
                pltpu.VMEM((2, size.row_slots * size.stride, LANES), F32),
                pltpu.VMEM((4, 2, rows, 2 * LANES), BF16),
                pltpu.VMEM((4, rows, 2 * LANES), F32),
                pltpu.VMEM((2, 2 * width, 2 * LANES), F32),
                pltpu.VMEM((2, SUB, 2 * LANES), F32),
                pltpu.VMEM((3, 6 * LANES, 2 * LANES), BF16),
                pltpu.VMEM((2, SUB, 2 * LANES), F32),
            ],
        ),
        out_shape=[
            jax.ShapeDtypeStruct((size.slots * size.both, 2 * LANES), F32),
            jax.ShapeDtypeStruct((2, 2, width + SUB, LANES), F32),
        ],
        compiler_params=pltpu.CompilerParams(vmem_limit_bytes=GRADIENT_VMEM),
        name="spectral_gradients",
    )(place, *fields, *consts, first_weight, second_weight, first_bias, second_bias)


def lat_back(size, place, s_modes, weight, part):
    width = weight.shape[-1]
    lat = lat_table(size, False).T.copy()
    lat[:, size.half :] *= -1.0
    table = jnp.asarray(four_way(lat))
    rows = size.batch * size.both
    steps = size.slots // size.batch // PARTS
    return pl.pallas_call(
        functools.partial(lat_back_kernel, size, width),
        grid_spec=pltpu.PrefetchScalarGridSpec(
            num_scalar_prefetch=1,
            grid=(steps,),
            in_specs=[
                pl.BlockSpec((rows, 2 * LANES), lambda i, at: (part * steps + i, 0)),
                pl.BlockSpec((2, 1, width, width), lambda i, at: (0, at[1], 0, 0)),
                whole_spec(table),
            ],
            out_specs=pl.BlockSpec((2, size.batch, size.row_slots, LANES), lambda i, at: (0, i, 0, 0)),
            scratch_shapes=[pltpu.VMEM((rows, 2 * LANES), F32), pltpu.VMEM((1, 6 * LANES, 2 * LANES), BF16)],
        ),
        out_shape=jax.ShapeDtypeStruct((2, size.slots // PARTS, size.row_slots, LANES), F32),
        compiler_params=pltpu.CompilerParams(vmem_limit_bytes=LAT_VMEM),
        name="lat_back",
    )(place, s_modes, weight, table)


def lon_back(size, width, v_parts):
    table = jnp.asarray(three_way(lon_table(size, False).T))
    field = pl.BlockSpec((2, size.slots // PARTS, LATS, LANES), lambda i: (0, 0, i, 0))
    return pl.pallas_call(
        functools.partial(lon_back_kernel, size, width),
        grid=(size.row_slots // LATS,),
        in_specs=[field] * PARTS + [whole_spec(table)],
        out_specs=pl.BlockSpec((size.cols * LATS // SUB, SUB, width), lambda i: (i, 0, 0)),
        out_shape=jax.ShapeDtypeStruct((size.rows * size.cols // SUB, SUB, width), F32),
        compiler_params=pltpu.CompilerParams(vmem_limit_bytes=LON_VMEM),
        name="lon_back",
    )(*v_parts, table)


def assemble(place, parts, width):
    count = len(parts)
    shapes = [(2, count, width, width)] * 2 + [(2, count, width)] * 2
    memory = pl.BlockSpec(memory_space=pltpu.VMEM)
    return pl.pallas_call(
        functools.partial(assemble_kernel, width, count),
        in_specs=[pl.BlockSpec(memory_space=pltpu.SMEM)] + [memory] * count,
        out_specs=[memory] * 4,
        out_shape=[jax.ShapeDtypeStruct(shape, F32) for shape in shapes],
        compiler_params=pltpu.CompilerParams(vmem_limit_bytes=LON_VMEM),
        name="assemble",
    )(place, *parts)


def crossed(value, axis, mask):
    count = lax.axis_size(axis)
    return lax.ppermute(value, axis, [(i, i ^ mask) for i in range(count)])


def whole_block(layer_input, grad_output, first_weight, first_bias, second_weight, second_bias):
    _, width, lat_rows, lon_cols = layer_input.shape
    size = Sizes(lat_rows, lon_cols)
    at_lat, at_lon = lax.axis_index("lat"), lax.axis_index("lon")
    place = jnp.stack([at_lat, at_lon] + [at_lon ^ x for x in range(lax.axis_size("lon"))])
    fields = [
        jnp.transpose(field, (0, 2, 3, 1)).reshape(-1, SUB, width) for field in (layer_input, grad_output)
    ]
    s_modes, partial = spectral_gradients(
        size, place, fields, first_weight, first_bias, second_weight, second_bias
    )
    matrices = partial.reshape(4, width + SUB, LANES)
    far = crossed(matrices, "lat", 1)
    v_first = lat_back(size, place, s_modes, first_weight, 0)
    far, v_first, s_modes = lax.optimization_barrier((far, v_first, s_modes))
    pair = matrices + far
    far = crossed(pair, "lat", 2)
    v_second = lat_back(size, place, s_modes, first_weight, 1)
    far, v_first, v_second = lax.optimization_barrier((far, v_first, v_second))
    own = pair + far
    chips = [crossed(own, "lon", mask) for mask in (2, 4, 6)]
    near = crossed(own, "lon", 1)
    out = lon_back(size, width, [v_first, v_second])
    chips, near, out = lax.optimization_barrier((chips, near, out))
    rest = [crossed(chip, "lon", 1) for chip in chips]
    parts = [own, near, chips[0], rest[0], chips[1], rest[1], chips[2], rest[2]]
    weight_one, weight_two, bias_one, bias_two = assemble(place, parts, width)
    grad_input = out.reshape(lat_rows * lon_cols, width).T.reshape(1, width, lat_rows, lon_cols)
    return (grad_input, weight_one, bias_one, weight_two, bias_two)


def tables(length, count, limit):
    first = jnp.arange(length, dtype=jnp.int32)[:, None]
    second = jnp.arange(count, dtype=jnp.int32)[None, :]
    angle = 2.0 * math.pi / length * (first * second % length).astype(jnp.float32)
    keeper = (second < limit).astype(jnp.float32) / math.sqrt(length)
    return (jnp.cos(angle) * keeper, jnp.sin(angle) * keeper)


def cotangent_weight(length, count):
    index = jnp.arange(count, dtype=jnp.int32)
    edge = (index == 0) | (2 * index == length)
    return jnp.where(edge, 1.0, 2.0).astype(jnp.float32)


def gelu_slope(value):
    inner = GELU_SCALE * (value + GELU_CUBE * value * value * value)
    tangent = jnp.tanh(inner)
    return 0.5 * (1.0 + tangent) + 0.5 * value * (1.0 - tangent * tangent) * GELU_SCALE * (
        1.0 + 3.0 * GELU_CUBE * value * value
    )


def complex_matrix(weight):
    real_part = weight[0]
    imag_part = weight[1]
    upper = jnp.stack([real_part, imag_part], axis=1)
    lower = jnp.stack([-imag_part, real_part], axis=1)
    return jnp.stack([upper, lower], axis=0)


def forward_mix(left, matrix):
    return jnp.einsum("psir,piqj->qsjr", left, matrix, precision=PRECISION)


def back_mix(left, matrix):
    return jnp.einsum("qsjr,piqj->psir", left, matrix, precision=PRECISION)


def weight_grad(left, right):
    total = jnp.einsum("psir,qsjr->piqj", left, right, precision=PRECISION)
    return jnp.stack(
        [total[0, :, 0, :] + total[1, :, 1, :], total[0, :, 1, :] - total[1, :, 0, :]]
    )


def bias_view(vector):
    return vector[:, None, :, None]


def block_backward(x_both, g_both, first_weight, first_bias, second_weight, second_bias):
    first_matrix = complex_matrix(first_weight)
    second_matrix = complex_matrix(second_weight)
    a_both = forward_mix(x_both, first_matrix) + bias_view(first_bias)
    o_both = jax.nn.gelu(a_both, approximate=True)
    z_both = forward_mix(o_both, second_matrix) + bias_view(second_bias)
    e_both = g_both * jnp.tanh(z_both / SHRINK) ** 2
    grad_w_two = weight_grad(o_both, e_both)
    grad_b_two = jnp.sum(e_both, axis=(1, 3))
    s_both = back_mix(e_both, second_matrix) * gelu_slope(a_both)
    grad_w_one = weight_grad(x_both, s_both)
    grad_b_one = jnp.sum(s_both, axis=(1, 3))
    d_both = back_mix(s_both, first_matrix)
    return d_both, (grad_w_one, grad_b_one, grad_w_two, grad_b_two)


def spread_block(layer_input, grad_output, first_weight, first_bias, second_weight, second_bias):
    lon_count = lax.axis_size("lon")
    samples, local_ch, lat_rows, lon_cols = layer_input.shape
    blocks, width = first_weight.shape[1], first_weight.shape[2]
    group = width // local_ch
    groups = [list(range(at, at + group)) for at in range(0, lon_count, group)]
    block = lax.axis_index("lon") // group
    kept_freqs = lon_cols // 2 + 1
    freq_slots = -(-kept_freqs // group) * group
    lon_cos, lon_sin = tables(lon_cols, freq_slots, kept_freqs)
    factor_row = cotangent_weight(lon_cols, freq_slots)[None, :]
    lon_table = jnp.stack([lon_cos, -lon_sin], axis=1)
    cot_table = jnp.stack([lon_cos * factor_row, -lon_sin * factor_row], axis=1)
    lon_back = jnp.stack([lon_cos.T, -lon_sin.T])
    lat_cos, lat_sin = tables(lat_rows, lat_rows, lat_rows)
    lat_table = jnp.stack(
        [jnp.stack([lat_cos, -lat_sin], axis=1), jnp.stack([lat_sin, lat_cos], axis=1)]
    )
    lat_back = jnp.stack(
        [jnp.stack([lat_cos, lat_sin], axis=1), jnp.stack([-lat_sin, lat_cos], axis=1)]
    )

    def spectrum(data, table):
        half = jnp.einsum("schw,wqk->qsckh", data, table, precision=PRECISION)
        full = jnp.einsum("psckh,phqm->qsckm", half, lat_table, precision=PRECISION)
        return full.reshape((2, samples, local_ch, freq_slots * lat_rows))

    def share(data, split, concat):
        if group == 1:
            return data
        return lax.all_to_all(
            data, "lon", split_axis=split, concat_axis=concat, axis_index_groups=groups, tiled=True
        )

    x_modes = share(spectrum(layer_input, lon_table), 3, 2)
    g_modes = share(spectrum(grad_output, cot_table), 3, 2)

    def mine(weight):
        return lax.dynamic_index_in_dim(weight, block, axis=1, keepdims=False)

    d_modes, partial_grads = block_backward(
        x_modes, g_modes, mine(first_weight), mine(first_bias), mine(second_weight), mine(second_bias)
    )
    flat_grads = jnp.concatenate([piece.reshape(-1) for piece in partial_grads])
    summed = lax.psum(flat_grads, "lat")
    if group > 1:
        summed = lax.psum(summed, "lon", axis_index_groups=groups)
    whole = lax.all_gather(summed, "lon", axis=0, tiled=False)[::group]
    stacked = share(d_modes, 2, 3)
    shape_five = (2, samples, local_ch, freq_slots, lat_rows)
    grad_input = jnp.einsum(
        "qsckh,qkw->schw",
        jnp.einsum("psckm,pmqh->qsckh", stacked.reshape(shape_five), lat_back, precision=PRECISION),
        lon_back,
        precision=PRECISION,
    )
    results = []
    offset = 0
    for piece in partial_grads:
        part = whole[:, offset : offset + piece.size].reshape((blocks,) + piece.shape)
        results.append(jnp.moveaxis(part, 0, 1))
        offset = offset + piece.size
    grad_w_one, grad_b_one, grad_w_two, grad_b_two = results
    return (grad_input, grad_w_one, grad_b_one, grad_w_two, grad_b_two)


def on_device(layer_input, grad_output, first_weight, first_bias, second_weight, second_bias):
    samples, local_ch, lat_rows, lon_cols = layer_input.shape
    width = first_weight.shape[2]
    one_device = samples == 1 and local_ch == width <= LANES and width % SUB == 0
    one_device = one_device and lax.axis_size("lat") == 4 and lax.axis_size("lon") == 8
    run = whole_block if one_device and Sizes(lat_rows, lon_cols).fits() else spread_block
    return run(layer_input, grad_output, first_weight, first_bias, second_weight, second_bias)


def solution(mesh):
    placed = (P("lat", "lon", None, None), P("lat", "lon", None, None), P(), P(), P(), P())
    return jax.shard_map(
        on_device,
        mesh=mesh,
        in_specs=placed,
        out_specs=(P("lat", "lon", None, None), P(), P(), P(), P()),
        check_vma=False,
    )
```

```python
import functools
import math

import jax
import jax.numpy as jnp
import ml_dtypes
import numpy as np
from jax import lax
from jax.experimental import pallas as pl
from jax.experimental.pallas import tpu as pltpu
from jax.sharding import PartitionSpec as P

SHRINK = 0.01
GELU_SCALE = math.sqrt(2.0 / math.pi)
GELU_CUBE = 0.044715
PRECISION = lax.Precision.HIGH
LANES = 128
SUB = 8
F32 = jnp.float32
BF16 = jnp.bfloat16
CHUNK = 4
LATS = 16
BAND_MOST = 18
PARTS = 2
GRADIENT_VMEM = 54 << 20
LAT_VMEM = 46 << 20
LON_VMEM = 24 << 20


def round_up(value, unit):
    return -(-value // unit) * unit


def halves(table):
    high = table.astype(ml_dtypes.bfloat16)
    low = (table - high.astype(np.float64)).astype(ml_dtypes.bfloat16)
    return high, low


def split(value):
    high = value.astype(BF16)
    return high, (value - high.astype(F32)).astype(BF16)


def dot(left, right):
    return jnp.dot(left, right, preferred_element_type=F32)


def side_by_side(left, right):
    return jnp.concatenate([left, right], axis=1)


def trig(length, count):
    first = np.arange(count)[:, None]
    second = np.arange(length)[None, :]
    angle = 2.0 * np.pi / length * (first * second % length)
    return np.cos(angle) / math.sqrt(length), np.sin(angle) / math.sqrt(length)


class Sizes:
    def __init__(self, rows, cols):
        self.rows, self.cols = rows, cols
        self.pairs = rows // 2 + 1
        self.half = round_up(self.pairs, SUB)
        self.both = 2 * self.half
        self.freqs = cols // 2 + 1
        self.slots = round_up(self.freqs, 16)
        self.stride = round_up(2 * self.slots, 2 * SUB) + SUB
        self.row_slots = round_up(rows, 16)
        self.col_slots = round_up(cols, 16)
        self.band = max((n for n in range(2, BAND_MOST + 1, 2) if rows % n == 0 and n * cols % SUB == 0), default=0)
        self.batch = SUB

    def fits(self):
        return self.band > 0 and self.cols % 4 == 0


def lat_table(size, cotangent):
    cos, sin = trig(size.rows, size.pairs)
    if cotangent:
        own = np.array([2 * m % size.rows == 0 for m in range(size.pairs)])
        cos, sin = (part * np.where(own, 0.5, 1.0)[:, None] for part in (cos, sin))
    table = np.zeros((size.both, size.row_slots))
    table[: size.pairs, : size.rows] = cos
    table[size.half : size.half + size.pairs, : size.rows] = sin
    return table


def lon_table(size, cotangent):
    cos, sin = trig(size.cols, size.freqs)
    if cotangent:
        index = np.arange(size.freqs)
        factor = np.where((index == 0) | (2 * index == size.cols), 1.0, 2.0)[:, None]
        cos, sin = cos * factor, sin * factor
    table = np.zeros((2 * size.slots, size.col_slots))
    table[: size.freqs, : size.cols] = cos
    table[size.slots : size.slots + size.freqs, : size.cols] = sin
    return table


def four_way(table):
    high, low = halves(table)
    return np.concatenate([np.concatenate([high, high], 1), np.concatenate([low, low], 1)], 0)


def three_way(table):
    high, low = halves(table)
    return np.concatenate([high, low, high], 1)


def four_product(table_ref, data):
    two = dot(table_ref[...], jnp.concatenate(split(data), axis=0))
    count = two.shape[0] // 2
    return two[:count] + two[count:]


def three_product(table_ref, high, low):
    return dot(table_ref[...], jnp.concatenate([high, high, low], axis=0))


def mix(weight_ref, which, high, low):
    return dot(jnp.concatenate([high, low, high], axis=1), weight_ref[which])


def fill_matrix(out, width, real, imag, turned, scale=1.0):
    if turned:
        real, imag = real.T, imag.T
    real, imag = real * scale, imag * scale
    sign = -1.0 if turned else 1.0
    span = 2 * LANES
    for row, column, value in ((0, 0, real), (1, 1, real), (0, 1, sign * imag), (1, 0, -sign * imag)):
        high, low = split(value)
        columns = slice(column * LANES, column * LANES + width)
        for third, part in enumerate((high, high, low)):
            at = third * span + row * LANES
            out[at : at + width, columns] = part


def gradient_kernel(
    size, width, bands, batches, at_ref, x_ref, g_ref, tx_ref, tg_ref, fx_ref, fg_ref, wa_ref, wb_ref, ba_ref, bb_ref,
    s_ref, grad_ref, fold, spectra, keep, plain, total, bias_total, w_ref, b_ref,
):
    step = pl.program_id(0)
    cols, slots, both, half = size.cols, size.slots, size.both, size.half
    stride = size.stride
    lines = 2 * slots
    rows = size.batch * both

    @pl.when(step == 0)
    def _():
        fold[...] = jnp.zeros_like(fold)
        total[...] = jnp.zeros_like(total)
        bias_total[...] = jnp.zeros_like(bias_total)
        w_ref[...] = jnp.zeros_like(w_ref)
        b_ref[...] = jnp.zeros_like(b_ref)
        fill_matrix(w_ref.at[0], width, wa_ref[0, 0], wa_ref[1, 0], False)
        fill_matrix(w_ref.at[1], width, wb_ref[0, 0], wb_ref[1, 0], False, 1.0 / SHRINK)
        fill_matrix(w_ref.at[2], width, wb_ref[0, 0], wb_ref[1, 0], True)
        for layer, (bias, scale) in enumerate(((ba_ref, 1.0), (bb_ref, 1.0 / SHRINK))):
            for q in range(2):
                row = bias[q, pl.ds(at_ref[1], 1), :] * scale
                b_ref[layer, :, q * LANES : q * LANES + width] = jnp.broadcast_to(row, (SUB, width))
        for which in range(2):
            spectra[which, size.rows * stride :] = jnp.zeros(((size.row_slots - size.rows) * stride, LANES), F32)

    @pl.when(step < bands)
    def _():
        for which, (field, table) in enumerate(((x_ref, tx_ref), (g_ref, tg_ref))):
            data = field.reshape(size.band * cols, width)
            for pair in range(size.band // 2):
                slot = which * (size.band // 2) + pair
                for i in range(2):
                    at = (2 * pair + i) * cols
                    high, low = split(data[at : at + cols, :])
                    fold[slot, 0, :cols, i * LANES : i * LANES + width] = high
                    fold[slot, 1, :cols, i * LANES : i * LANES + width] = low
                out = three_product(table, fold[slot, 0], fold[slot, 1])
                for i in range(2):
                    base = pl.multiple_of((step * size.band + 2 * pair + i) * stride, SUB)
                    spectra[which, pl.ds(base, lines), :] = out[:, i * LANES : (i + 1) * LANES]

    @pl.when(step >= bands)
    def _():
        first = (step - bands) * size.batch
        span = CHUNK * both
        piece = 16

        def transform(chunk):
            for k in range(chunk * CHUNK, (chunk + 1) * CHUNK):
                at = k * both
                for which, table in enumerate((fx_ref, fg_ref)):
                    data = side_by_side(
                        spectra[which, pl.ds(first + k, size.row_slots, stride=stride), :],
                        spectra[which, pl.ds(first + k + slots, size.row_slots, stride=stride), :],
                    )
                    out = three_product(table, *split(data))
                    cos_one, cos_two = out[:half, :LANES], out[:half, LANES:]
                    sin_one, sin_two = out[half:, :LANES], out[half:, LANES:]
                    plus = side_by_side(cos_one - sin_two, -(cos_two + sin_one))
                    minus = side_by_side(cos_one + sin_two, sin_one - cos_two)
                    for part, value in ((0, plus), (1, minus)):
                        here = slice(at + part * half, at + (part + 1) * half)
                        if which == 0:
                            keep_split(0, here, value)
                        else:
                            plain[0, here] = value

        def keep_split(which, here, value):
            high, low = split(value)
            keep[which, 0, here] = high
            keep[which, 1, here] = low

        def multiply(which, chunk):
            here = slice(chunk * span, (chunk + 1) * span)
            plain[1 + which, here] = mix(w_ref, which, keep[which, 0, here], keep[which, 1, here])

        def pieces(chunk):
            return [slice(at, at + piece) for at in range(chunk * span, (chunk + 1) * span, piece)]

        def activate(chunk):
            for here in pieces(chunk):
                a = plain[1, here] + b_ref[0, :1]
                square = a * a
                tangent = jnp.tanh(a * (GELU_SCALE + (GELU_SCALE * GELU_CUBE) * square))
                share = 0.5 * tangent + 0.5
                o = a * share
                plain[1, here] = share + (o - o * share) * (
                    2.0 * GELU_SCALE + (6.0 * GELU_SCALE * GELU_CUBE) * square
                )
                keep_split(1, here, o)

        def gate(chunk):
            sums = jnp.zeros((SUB, 2 * LANES), F32)
            for here in pieces(chunk):
                tangent = jnp.tanh(plain[2, here] + b_ref[1, :1])
                e = plain[0, here] * (tangent * tangent)
                for i in range(0, piece, SUB):
                    sums = sums + e[i : i + SUB]
                keep_split(2, here, e)
            bias_total[1] += sums

        def slope(chunk):
            sums = jnp.zeros((SUB, 2 * LANES), F32)
            for here in pieces(chunk):
                value = plain[3, here] * plain[1, here]
                s_ref[here] = value
                for i in range(0, piece, SUB):
                    sums = sums + value[i : i + SUB]
                keep_split(3, here, value)
            bias_total[0] += sums

        def turned(which):
            parts = [keep[which, i].T for i in range(2)]
            return [jnp.concatenate([part[:width], part[LANES : LANES + width]], axis=0) for part in parts]

        def weight_grad(layer, left, right):
            high, low = turned(left)
            total[layer] += dot(
                jnp.concatenate([high, low, high], axis=1),
                jnp.concatenate([keep[right, 0], keep[right, 0], keep[right, 1]], axis=0),
            )

        count = size.batch // CHUNK
        for t in range(count + 3):
            if t < count:
                transform(t)
                multiply(0, t)
            if 0 <= t - 1 < count:
                activate(t - 1)
                multiply(1, t - 1)
            if 0 <= t - 2 < count:
                gate(t - 2)
                multiply(2, t - 2)
            if 0 <= t - 3 < count:
                slope(t - 3)
        weight_grad(1, 1, 2)
        weight_grad(0, 0, 3)

    @pl.when(step == bands + batches - 1)
    def _():
        for layer in range(2):
            upper = total[layer, :width]
            lower = total[layer, width:]
            grad_ref[layer, 0, :width] = upper[:, :LANES] + lower[:, LANES:]
            grad_ref[layer, 1, :width] = upper[:, LANES:] - lower[:, :LANES]
            bias = jnp.broadcast_to(jnp.sum(bias_total[layer], axis=0, keepdims=True), (SUB, 2 * LANES))
            grad_ref[layer, 0, width:] = bias[:, :LANES]
            grad_ref[layer, 1, width:] = bias[:, LANES:]


def lat_back_kernel(size, width, at_ref, s_ref, wa_ref, f_ref, v_ref, plain, w_ref):
    both, half = size.both, size.half
    span = CHUNK * both

    @pl.when(pl.program_id(0) == 0)
    def _():
        w_ref[...] = jnp.zeros_like(w_ref)
        fill_matrix(w_ref.at[0], width, wa_ref[0, 0], wa_ref[1, 0], True)

    def multiply(chunk):
        here = slice(chunk * span, (chunk + 1) * span)
        plain[here] = mix(w_ref, 0, *split(s_ref[here]))

    def transform(chunk):
        for k in range(chunk * CHUNK, (chunk + 1) * CHUNK):
            at = k * both
            plus, minus = plain[at : at + half], plain[at + half : at + both]
            add, sub = plus + minus, plus - minus
            data = jnp.concatenate(
                [
                    side_by_side(add[:, :LANES], -add[:, LANES:]),
                    side_by_side(sub[:, LANES:], sub[:, :LANES]),
                ],
                axis=0,
            )
            out = three_product(f_ref, *split(data))
            for q in range(2):
                v_ref[q, k] = out[:, q * LANES : (q + 1) * LANES]

    count = size.batch // CHUNK
    for t in range(count + 1):
        if t < count:
            multiply(t)
        if t > 0:
            transform(t - 1)


def lon_back_kernel(size, width, *refs):
    v_refs, (t_ref, out_ref) = refs[:PARTS], refs[PARTS:]
    cols = size.cols
    lines = size.slots // PARTS
    flat = out_ref.reshape(LATS * cols, width)
    rows = [ref.reshape(2 * lines * LATS, LANES) for ref in v_refs]
    for pair in range(LATS // 2):
        data = side_by_side(
            *(
                jnp.concatenate(
                    [
                        part[pl.ds(q * lines * LATS + 2 * pair + i, lines, stride=LATS), :]
                        for q in range(2)
                        for part in rows
                    ],
                    axis=0,
                )
                for i in range(2)
            )
        )
        out = three_product(t_ref, *split(data))
        for i in range(2):
            at = (2 * pair + i) * cols
            flat[at : at + cols, :] = out[:cols, i * LANES : i * LANES + width]


def assemble_kernel(width, count, at_ref, *refs):
    parts, (wa_ref, wb_ref, ba_ref, bb_ref) = refs[:count], refs[count:]
    for l, (weight, bias) in enumerate(((wa_ref, ba_ref), (wa_ref, ba_ref), (wb_ref, bb_ref), (wb_ref, bb_ref))):
        for x in range(count):
            block = at_ref[2 + x]
            weight[l % 2, block] = parts[x][l, :width, :width]
            bias[l % 2, pl.ds(block, 1), :] = parts[x][l, width : width + 1, :width]


def whole_spec(array):
    zeros = (0,) * array.ndim
    return pl.BlockSpec(array.shape, lambda *_: zeros)


def spectral_gradients(size, place, fields, first_weight, first_bias, second_weight, second_bias):
    width = first_weight.shape[-1]
    tables = [three_way(lon_table(size, which)) for which in (False, True)]
    tables += [three_way(lat_table(size, which)) for which in (False, True)]
    consts = [jnp.asarray(table) for table in tables]
    weight = pl.BlockSpec((2, 1, width, width), lambda i, at: (0, at[1], 0, 0))
    bias = whole_spec(first_bias)
    bands, batches = size.rows // size.band, size.slots // size.batch
    rows = size.batch * size.both
    field = pl.BlockSpec((size.band * size.cols // SUB, SUB, width), lambda i, at: (jnp.minimum(i, bands - 1), 0, 0))
    return pl.pallas_call(
        functools.partial(gradient_kernel, size, width, bands, batches),
        grid_spec=pltpu.PrefetchScalarGridSpec(
            num_scalar_prefetch=1,
            grid=(bands + batches,),
            in_specs=[field, field] + [whole_spec(const) for const in consts] + [weight, weight, bias, bias],
            out_specs=[
                pl.BlockSpec((rows, 2 * LANES), lambda i, at: (jnp.maximum(i - bands, 0), 0)),
                pl.BlockSpec((2, 2, width + SUB, LANES), lambda i, at: (0, 0, 0, 0)),
            ],
            scratch_shapes=[
                pltpu.VMEM((size.band, 2, size.col_slots, 2 * LANES), BF16),
                pltpu.VMEM((2, size.row_slots * size.stride, LANES), F32),
                pltpu.VMEM((4, 2, rows, 2 * LANES), BF16),
                pltpu.VMEM((4, rows, 2 * LANES), F32),
                pltpu.VMEM((2, 2 * width, 2 * LANES), F32),
                pltpu.VMEM((2, SUB, 2 * LANES), F32),
                pltpu.VMEM((3, 6 * LANES, 2 * LANES), BF16),
                pltpu.VMEM((2, SUB, 2 * LANES), F32),
            ],
        ),
        out_shape=[
            jax.ShapeDtypeStruct((size.slots * size.both, 2 * LANES), F32),
            jax.ShapeDtypeStruct((2, 2, width + SUB, LANES), F32),
        ],
        compiler_params=pltpu.CompilerParams(vmem_limit_bytes=GRADIENT_VMEM),
        name="spectral_gradients",
    )(place, *fields, *consts, first_weight, second_weight, first_bias, second_bias)


def lat_back(size, place, s_modes, weight, part):
    width = weight.shape[-1]
    lat = lat_table(size, False).T.copy()
    lat[:, size.half :] *= -1.0
    table = jnp.asarray(three_way(lat))
    rows = size.batch * size.both
    steps = size.slots // size.batch // PARTS
    return pl.pallas_call(
        functools.partial(lat_back_kernel, size, width),
        grid_spec=pltpu.PrefetchScalarGridSpec(
            num_scalar_prefetch=1,
            grid=(steps,),
            in_specs=[
                pl.BlockSpec((rows, 2 * LANES), lambda i, at: (part * steps + i, 0)),
                pl.BlockSpec((2, 1, width, width), lambda i, at: (0, at[1], 0, 0)),
                whole_spec(table),
            ],
            out_specs=pl.BlockSpec((2, size.batch, size.row_slots, LANES), lambda i, at: (0, i, 0, 0)),
            scratch_shapes=[pltpu.VMEM((rows, 2 * LANES), F32), pltpu.VMEM((1, 6 * LANES, 2 * LANES), BF16)],
        ),
        out_shape=jax.ShapeDtypeStruct((2, size.slots // PARTS, size.row_slots, LANES), F32),
        compiler_params=pltpu.CompilerParams(vmem_limit_bytes=LAT_VMEM),
        name="lat_back",
    )(place, s_modes, weight, table)


def lon_back(size, width, v_parts):
    table = jnp.asarray(three_way(lon_table(size, False).T))
    field = pl.BlockSpec((2, size.slots // PARTS, LATS, LANES), lambda i: (0, 0, i, 0))
    return pl.pallas_call(
        functools.partial(lon_back_kernel, size, width),
        grid=(size.row_slots // LATS,),
        in_specs=[field] * PARTS + [whole_spec(table)],
        out_specs=pl.BlockSpec((size.cols * LATS // SUB, SUB, width), lambda i: (i, 0, 0)),
        out_shape=jax.ShapeDtypeStruct((size.rows * size.cols // SUB, SUB, width), F32),
        compiler_params=pltpu.CompilerParams(vmem_limit_bytes=LON_VMEM),
        name="lon_back",
    )(*v_parts, table)


def assemble(place, parts, width):
    count = len(parts)
    shapes = [(2, count, width, width)] * 2 + [(2, count, width)] * 2
    memory = pl.BlockSpec(memory_space=pltpu.VMEM)
    return pl.pallas_call(
        functools.partial(assemble_kernel, width, count),
        in_specs=[pl.BlockSpec(memory_space=pltpu.SMEM)] + [memory] * count,
        out_specs=[memory] * 4,
        out_shape=[jax.ShapeDtypeStruct(shape, F32) for shape in shapes],
        compiler_params=pltpu.CompilerParams(vmem_limit_bytes=LON_VMEM),
        name="assemble",
    )(place, *parts)


def crossed(value, axis, mask):
    count = lax.axis_size(axis)
    return lax.ppermute(value, axis, [(i, i ^ mask) for i in range(count)])


def whole_block(layer_input, grad_output, first_weight, first_bias, second_weight, second_bias):
    _, width, lat_rows, lon_cols = layer_input.shape
    size = Sizes(lat_rows, lon_cols)
    at_lat, at_lon = lax.axis_index("lat"), lax.axis_index("lon")
    place = jnp.stack([at_lat, at_lon] + [at_lon ^ x for x in range(lax.axis_size("lon"))])
    fields = [
        jnp.transpose(field, (0, 2, 3, 1)).reshape(-1, SUB, width) for field in (layer_input, grad_output)
    ]
    s_modes, partial = spectral_gradients(
        size, place, fields, first_weight, first_bias, second_weight, second_bias
    )
    matrices = partial.reshape(4, width + SUB, LANES)
    far = crossed(matrices, "lat", 1)
    v_first = lat_back(size, place, s_modes, first_weight, 0)
    far, v_first, s_modes = lax.optimization_barrier((far, v_first, s_modes))
    pair = matrices + far
    far = crossed(pair, "lat", 2)
    v_second = lat_back(size, place, s_modes, first_weight, 1)
    far, v_first, v_second = lax.optimization_barrier((far, v_first, v_second))
    own = pair + far
    chips = [crossed(own, "lon", mask) for mask in (2, 4, 6)]
    near = crossed(own, "lon", 1)
    out = lon_back(size, width, [v_first, v_second])
    chips, near, out = lax.optimization_barrier((chips, near, out))
    rest = [crossed(chip, "lon", 1) for chip in chips]
    parts = [own, near, chips[0], rest[0], chips[1], rest[1], chips[2], rest[2]]
    weight_one, weight_two, bias_one, bias_two = assemble(place, parts, width)
    grad_input = out.reshape(lat_rows * lon_cols, width).T.reshape(1, width, lat_rows, lon_cols)
    return (grad_input, weight_one, bias_one, weight_two, bias_two)


def tables(length, count, limit):
    first = jnp.arange(length, dtype=jnp.int32)[:, None]
    second = jnp.arange(count, dtype=jnp.int32)[None, :]
    angle = 2.0 * math.pi / length * (first * second % length).astype(jnp.float32)
    keeper = (second < limit).astype(jnp.float32) / math.sqrt(length)
    return (jnp.cos(angle) * keeper, jnp.sin(angle) * keeper)


def cotangent_weight(length, count):
    index = jnp.arange(count, dtype=jnp.int32)
    edge = (index == 0) | (2 * index == length)
    return jnp.where(edge, 1.0, 2.0).astype(jnp.float32)


def gelu_slope(value):
    inner = GELU_SCALE * (value + GELU_CUBE * value * value * value)
    tangent = jnp.tanh(inner)
    return 0.5 * (1.0 + tangent) + 0.5 * value * (1.0 - tangent * tangent) * GELU_SCALE * (
        1.0 + 3.0 * GELU_CUBE * value * value
    )


def complex_matrix(weight):
    real_part = weight[0]
    imag_part = weight[1]
    upper = jnp.stack([real_part, imag_part], axis=1)
    lower = jnp.stack([-imag_part, real_part], axis=1)
    return jnp.stack([upper, lower], axis=0)


def forward_mix(left, matrix):
    return jnp.einsum("psir,piqj->qsjr", left, matrix, precision=PRECISION)


def back_mix(left, matrix):
    return jnp.einsum("qsjr,piqj->psir", left, matrix, precision=PRECISION)


def weight_grad(left, right):
    total = jnp.einsum("psir,qsjr->piqj", left, right, precision=PRECISION)
    return jnp.stack(
        [total[0, :, 0, :] + total[1, :, 1, :], total[0, :, 1, :] - total[1, :, 0, :]]
    )


def bias_view(vector):
    return vector[:, None, :, None]


def block_backward(x_both, g_both, first_weight, first_bias, second_weight, second_bias):
    first_matrix = complex_matrix(first_weight)
    second_matrix = complex_matrix(second_weight)
    a_both = forward_mix(x_both, first_matrix) + bias_view(first_bias)
    o_both = jax.nn.gelu(a_both, approximate=True)
    z_both = forward_mix(o_both, second_matrix) + bias_view(second_bias)
    e_both = g_both * jnp.tanh(z_both / SHRINK) ** 2
    grad_w_two = weight_grad(o_both, e_both)
    grad_b_two = jnp.sum(e_both, axis=(1, 3))
    s_both = back_mix(e_both, second_matrix) * gelu_slope(a_both)
    grad_w_one = weight_grad(x_both, s_both)
    grad_b_one = jnp.sum(s_both, axis=(1, 3))
    d_both = back_mix(s_both, first_matrix)
    return d_both, (grad_w_one, grad_b_one, grad_w_two, grad_b_two)


def spread_block(layer_input, grad_output, first_weight, first_bias, second_weight, second_bias):
    lon_count = lax.axis_size("lon")
    samples, local_ch, lat_rows, lon_cols = layer_input.shape
    blocks, width = first_weight.shape[1], first_weight.shape[2]
    group = width // local_ch
    groups = [list(range(at, at + group)) for at in range(0, lon_count, group)]
    block = lax.axis_index("lon") // group
    kept_freqs = lon_cols // 2 + 1
    freq_slots = -(-kept_freqs // group) * group
    lon_cos, lon_sin = tables(lon_cols, freq_slots, kept_freqs)
    factor_row = cotangent_weight(lon_cols, freq_slots)[None, :]
    lon_table = jnp.stack([lon_cos, -lon_sin], axis=1)
    cot_table = jnp.stack([lon_cos * factor_row, -lon_sin * factor_row], axis=1)
    lon_back = jnp.stack([lon_cos.T, -lon_sin.T])
    lat_cos, lat_sin = tables(lat_rows, lat_rows, lat_rows)
    lat_table = jnp.stack(
        [jnp.stack([lat_cos, -lat_sin], axis=1), jnp.stack([lat_sin, lat_cos], axis=1)]
    )
    lat_back = jnp.stack(
        [jnp.stack([lat_cos, lat_sin], axis=1), jnp.stack([-lat_sin, lat_cos], axis=1)]
    )

    def spectrum(data, table):
        half = jnp.einsum("schw,wqk->qsckh", data, table, precision=PRECISION)
        full = jnp.einsum("psckh,phqm->qsckm", half, lat_table, precision=PRECISION)
        return full.reshape((2, samples, local_ch, freq_slots * lat_rows))

    def share(data, split, concat):
        if group == 1:
            return data
        return lax.all_to_all(
            data, "lon", split_axis=split, concat_axis=concat, axis_index_groups=groups, tiled=True
        )

    x_modes = share(spectrum(layer_input, lon_table), 3, 2)
    g_modes = share(spectrum(grad_output, cot_table), 3, 2)

    def mine(weight):
        return lax.dynamic_index_in_dim(weight, block, axis=1, keepdims=False)

    d_modes, partial_grads = block_backward(
        x_modes, g_modes, mine(first_weight), mine(first_bias), mine(second_weight), mine(second_bias)
    )
    flat_grads = jnp.concatenate([piece.reshape(-1) for piece in partial_grads])
    summed = lax.psum(flat_grads, "lat")
    if group > 1:
        summed = lax.psum(summed, "lon", axis_index_groups=groups)
    whole = lax.all_gather(summed, "lon", axis=0, tiled=False)[::group]
    stacked = share(d_modes, 2, 3)
    shape_five = (2, samples, local_ch, freq_slots, lat_rows)
    grad_input = jnp.einsum(
        "qsckh,qkw->schw",
        jnp.einsum("psckm,pmqh->qsckh", stacked.reshape(shape_five), lat_back, precision=PRECISION),
        lon_back,
        precision=PRECISION,
    )
    results = []
    offset = 0
    for piece in partial_grads:
        part = whole[:, offset : offset + piece.size].reshape((blocks,) + piece.shape)
        results.append(jnp.moveaxis(part, 0, 1))
        offset = offset + piece.size
    grad_w_one, grad_b_one, grad_w_two, grad_b_two = results
    return (grad_input, grad_w_one, grad_b_one, grad_w_two, grad_b_two)


def on_device(layer_input, grad_output, first_weight, first_bias, second_weight, second_bias):
    samples, local_ch, lat_rows, lon_cols = layer_input.shape
    width = first_weight.shape[2]
    one_device = samples == 1 and local_ch == width <= LANES and width % SUB == 0
    one_device = one_device and lax.axis_size("lat") == 4 and lax.axis_size("lon") == 8
    run = whole_block if one_device and Sizes(lat_rows, lon_cols).fits() else spread_block
    return run(layer_input, grad_output, first_weight, first_bias, second_weight, second_bias)


def solution(mesh):
    placed = (P("lat", "lon", None, None), P("lat", "lon", None, None), P(), P(), P(), P())
    return jax.shard_map(
        on_device,
        mesh=mesh,
        in_specs=placed,
        out_specs=(P("lat", "lon", None, None), P(), P(), P(), P()),
        check_vma=False,
    )
```
